32 devices in a mesh: lat: 4 (over y, x), lon: 8 (over z, core).
Axes of the slice: x: 2, y: 2, z: 4, core: 2. Of those that a mesh axis runs over, the one named last changes fastest.
Arguments:
- cotangent: float32 [40, 2, 192, 1024], P(None, None, 'lat', 'lon'), may hold values from -6 to 6
- u_transport: float32 [40, 192, 1024], P(None, 'lat', 'lon'), may hold values from -0.2 to 0.2
- v_transport: float32 [40, 192, 1024], P(None, 'lat', 'lon'), may hold values from -0.2 to 0.2
- diffusivity: float32 [40, 192, 1024], P(None, 'lat', 'lon'), may hold values from 0.05 to 160
- land_sea: int32 [40, 192, 1024], P(None, 'lat', 'lon'), may hold values from 0 to 1
- bottom_level: int32 [192, 1024], P('lat', 'lon'), may hold values from 20 to 40
- partner: int32 [1024], P('lon'), may hold values from 0 to 1023, as said below
Outputs:
- adjoint: float32 [40, 2, 192, 1024], P(None, None, 'lat', 'lon')
The draws below stay inside these ranges and needn't reach their ends.
Inputs may be any that keep to these rules, and one draw needn't show every extreme that they name: partner is a permutation with partner[partner[i]] == i; it pairs every column of longitude sector s (columns s * 128 to (s + 1) * 128 - 1) with some column of sector 1024 // 128 - 1 - s, in an order drawn for each pair of sectors.
All inputs are finite; a program needn't handle non-finite values.
Results may differ from the reference program's by a relative error of at most 0.000067.
Values sent between devices are 32-bit elements; how exact they have to be, the bound alone decides.
A program may use at most 128 MiB of HBM per device.

```python
import jax
import jax.numpy as jnp
from jax import lax

K = 40
CX = 128
NY = 192
NX = 1024


def draw_partner(key, part):
    sectors = NX // CX
    pair_count = sectors // 2
    keys = jax.random.split(key, pair_count)
    orders = jax.vmap(lambda one_key: jax.random.permutation(one_key, CX))(keys).astype(jnp.int32)
    inverse_orders = jnp.argsort(orders, axis=1, stable=True).astype(jnp.int32)
    pair_ids = jnp.arange(pair_count, dtype=jnp.int32)[:, None]
    lower_part = (sectors - 1 - pair_ids) * CX + orders
    upper_part = pair_ids * CX + inverse_orders
    upper_part = upper_part[::-1]
    return jnp.concatenate([lower_part.reshape(-1), upper_part.reshape(-1)]).astype(jnp.int32)


def open_columns(key):
    picks = jax.random.randint(jax.random.fold_in(key, 7), (NY, NX // 8), 0, 3)
    return jnp.repeat(picks == 0, 8, axis=1)


def draw_land_sea(key, part):
    opened = open_columns(key)
    scattered = jax.random.randint(jax.random.fold_in(key, 11), (K, NY, NX), 0, 8) != 0
    return jnp.where(opened[None], 1, scattered.astype(jnp.int32)).astype(jnp.int32)


def draw_bottom_level(key, part):
    opened = open_columns(key)
    levels = jax.random.randint(jax.random.fold_in(key, 13), (NY, NX), K // 2, K + 1)
    return jnp.where(opened, K, levels).astype(jnp.int32)


def draw_diffusivity(key, part):
    opened = open_columns(key)
    first = jax.random.uniform(jax.random.fold_in(key, 17), (K, NY, NX), jnp.float32)
    second = jax.random.uniform(jax.random.fold_in(key, 19), (K, NY, NX), jnp.float32)
    shallow = 0.05 * jnp.exp(first * jnp.log(100.0))
    strong = 8.0 * jnp.exp(second * jnp.log(10.0))
    return jnp.where(opened[None], strong, shallow).astype(jnp.float32)


def steps_of(rng, extent, cuts, low, largest):
    def one(axis_at, parts):
        draws = jax.random.uniform(jax.random.fold_in(jax.random.fold_in(rng, 6), axis_at), (parts,), jnp.float32, low / len(cuts), largest / len(cuts))
        return jnp.repeat(jnp.exp(draws), extent[axis_at] // parts).reshape((-1,) + (1,) * (len(extent) - axis_at - 1))

    loudness = one(*cuts[0])
    for cut in cuts[1:]:
        loudness = loudness * one(*cut)
    return loudness


def centred(rng, extent, deviation, reach, cuts=(), kind=jnp.bfloat16):
    factor_of = steps_of(rng, extent, cuts, -0.22, 0.18) if cuts else 1.0
    values = jax.random.normal(rng, extent, jnp.float32) * deviation * factor_of
    return jnp.minimum(jnp.maximum(values, -reach), reach).astype(kind)


def setup_inputs(seed: int = 0) -> dict:
    streams_of = jax.random.split(jax.random.key(seed), 8)
    return {
        "cotangent": centred(streams_of[0], (K, 2, NY, NX), 1.0, 6.0, ((2, 4), (3, 8)), jnp.float32),
        "u_transport": jnp.clip(jax.random.uniform(streams_of[1], (K, NY, NX), jnp.float32, -0.2, 0.2) * steps_of(streams_of[1], (K, NY, NX), ((1, 4), (2, 8)), -0.4, 0.0), -0.2, 0.2),
        "v_transport": jnp.clip(jax.random.uniform(streams_of[2], (K, NY, NX), jnp.float32, -0.2, 0.2) * steps_of(streams_of[2], (K, NY, NX), ((1, 4), (2, 8)), -0.4, 0.0), -0.2, 0.2),
        "diffusivity": draw_diffusivity(jax.random.fold_in(streams_of[7], 71), 0),
        "land_sea": draw_land_sea(jax.random.fold_in(streams_of[7], 71), 0),
        "bottom_level": draw_bottom_level(jax.random.fold_in(streams_of[7], 71), 0),
        "partner": draw_partner(jax.random.fold_in(streams_of[7], 71), 0),
    }


LATERAL_MIX = 0.15
SALT_RATIO = 0.5

def wet_field(land_sea, bottom_level):
    level_ids = lax.broadcasted_iota(jnp.int32, land_sea.shape, 0)
    return (land_sea * (level_ids < bottom_level[None]).astype(jnp.int32)).astype(jnp.float32)

def factor_bands(lower_band, upper_band, diagonal):

    def sweep(previous, items):
        lower_item, upper_item, diagonal_item = items
        inverse = 1.0 / (diagonal_item - lower_item * previous)
        current = upper_item * inverse
        return (current, (current, inverse))
    _, (ratios, inverses) = lax.scan(sweep, jnp.zeros_like(diagonal[0]), (lower_band, upper_band, diagonal))
    return (ratios, inverses)

def solve_columns(rhs_field, lower_band, ratios, inverses):

    def downward(previous, items):
        rhs_item, lower_item, inverse = items
        current = (rhs_item - lower_item * previous) * inverse
        return (current, current)
    _, middles = lax.scan(downward, jnp.zeros_like(rhs_field[0]), (rhs_field, lower_band, inverses))

    def upward(following, items):
        middle, ratio_item = items
        current = middle - ratio_item * following
        return (current, current)
    _, result = lax.scan(upward, jnp.zeros_like(rhs_field[0]), (middles, ratios), reverse=True)
    return result

def lateral(field, u_transport, v_transport, wet, partner):
    wet_both = wet[:, None]
    u_both = u_transport[:, None]
    v_both = v_transport[:, None]
    east_value = jnp.roll(field, -1, axis=3)
    east_face = wet_both * jnp.roll(wet_both, -1, axis=3)
    flux_east = east_face * (jnp.maximum(u_both, 0.0) * field + jnp.minimum(u_both, 0.0) * east_value)
    mix_east = LATERAL_MIX * east_face * (east_value - field)
    ghost = jnp.take(wet_both[:, :, -1, :] * field[:, :, -1, :], partner, axis=2)
    north_value = jnp.concatenate([field[:, :, 1:, :], ghost[:, :, None, :]], axis=2)
    north_wet = jnp.concatenate([wet_both[:, :, 1:, :], jnp.ones_like(wet_both[:, :, :1, :])], axis=2)
    north_face = wet_both * north_wet
    flux_north = north_face * (jnp.maximum(v_both, 0.0) * field + jnp.minimum(v_both, 0.0) * north_value)
    mix_north = LATERAL_MIX * north_face * (north_value - field)
    flux_west = jnp.roll(flux_east, 1, axis=3)
    mix_west = jnp.roll(mix_east, 1, axis=3)
    zero_row = jnp.zeros_like(field[:, :, :1, :])
    flux_south = jnp.concatenate([zero_row, flux_north[:, :, :-1, :]], axis=2)
    mix_south = jnp.concatenate([zero_row, mix_north[:, :, :-1, :]], axis=2)
    total = field - flux_east + flux_west - flux_north + flux_south + mix_east - mix_west + mix_north - mix_south
    return wet_both * total

def reference(cotangent, u_transport, v_transport, diffusivity, land_sea, bottom_level, partner):
    wet = wet_field(land_sea, bottom_level)
    lower_one = -diffusivity * jnp.concatenate([jnp.zeros_like(wet[:1]), wet[:-1] * wet[1:]], axis=0)
    scales = jnp.array([1.0, SALT_RATIO], jnp.float32)[None, :, None, None]
    lower_band = lower_one[:, None] * scales
    upper_band = jnp.concatenate([lower_band[1:], jnp.zeros_like(lower_band[:1])], axis=0)
    ratios, inverses = factor_bands(lower_band, upper_band, 1.0 - lower_band - upper_band)

    def one_step(field):
        return solve_columns(lateral(field, u_transport, v_transport, wet, partner), lower_band, ratios, inverses)

    def two_steps(field):
        return one_step(one_step(field))
    _, pullback = jax.vjp(two_steps, jnp.zeros_like(cotangent))
    return pullback(cotangent)[0]
```

```python
import functools

import jax
import jax.numpy as jnp
from jax import lax
from jax.experimental import pallas as pl
from jax.experimental.pallas import tpu as pltpu
from jax.sharding import PartitionSpec as P

LATERAL_MIX = 0.15
SALT_RATIO = 0.5
UNROLL = 40
W_UNROLL = 20
UP_CUT = 1
ROW_PARTS = 5
RATIOS = (1.0, SALT_RATIO)
NORTH, SOUTH = range(2)
EAST, WEST = range(2)
CHUNKS = 5
PAD = 8


def kernel_body(
    cot_hbm, u_hbm, v_hbm, diff_hbm, land_hbm, bottom_hbm, partner_hbm, out,
    cot, u, v, diff, land, bottom, partner, wet, lean_v, big_q, big_i, x_field, z_field,
    c_mid, c_east, c_west, c_north, c_south, c_edge,
    row_send, row_recv, col_send, col_recv, north_rows,
    in_sem, row_send_sem, row_recv_sem, col_send_sem, col_recv_sem,
):
    levels, rows, cols = u.shape
    per_chunk = levels // CHUNKS
    lat, lon = lax.axis_index("lat"), lax.axis_index("lon")
    lats, lons = lax.axis_size("lat"), lax.axis_size("lon")
    is_top = lat == lats - 1
    has_south = lat > 0
    mirror = lons - 1 - lon
    east = (lat, lax.rem(lon + 1, lons))
    west = (lat, lax.rem(lon + lons - 1, lons))
    north = (jnp.where(is_top, lat, lat + 1), jnp.where(is_top, mirror, lon))
    south = (jnp.maximum(lat - 1, 0), lon)
    north_slot = jnp.where(is_top, NORTH, SOUTH)

    def signal(device):
        pl.semaphore_signal(
            barrier, inc=1, device_id=device, device_id_type=pl.DeviceIdType.MESH
        )

    barrier = pltpu.get_barrier_semaphore()
    signal(east)
    signal(west)
    signal(north)

    @pl.when(has_south)
    def _():
        signal(south)

    def load_whole(source, target, index):
        return pltpu.make_async_copy(source, target, in_sem.at[index, 0])

    def load_part(source, target, index, part):
        piece = pl.ds(part * per_chunk, per_chunk)
        return pltpu.make_async_copy(source.at[piece], target.at[piece], in_sem.at[index, part])

    whole = [load_whole(bottom_hbm, bottom, 0), load_whole(partner_hbm, partner, 6)]
    first = [
        [load_part(s, t, i, part) for s, t, i in ((land_hbm, land, 1), (diff_hbm, diff, 4), (cot_hbm, cot, 5))]
        for part in range(CHUNKS)
    ]
    second = [
        [load_part(s, t, i, part) for s, t, i in ((u_hbm, u, 2), (v_hbm, v, 3))]
        for part in range(CHUNKS)
    ]
    for copies in [whole] + first + second:
        for copy in copies:
            copy.start()

    lane = lax.broadcasted_iota(jnp.int32, (rows, cols), 1)
    row = lax.broadcasted_iota(jnp.int32, (rows, cols), 0)
    row_last = row == rows - 1
    lane_first, lane_last = lane == 0, lane == cols - 1
    lane_even = lax.rem(lane, 2) == 0
    zero = jnp.minimum(lat, 0)
    here = pl.ds(PAD, rows)
    one_north = pl.ds(PAD + 1 + zero, rows)
    one_south = pl.ds(PAD - 1 + zero, rows)
    row_low = lax.broadcasted_iota(jnp.int32, (8, cols), 0)
    low_first, low_last = row_low == 0, row_low == 7

    parts = row_send_sem.shape[2]
    part_rows = 2 * levels // parts

    def row_piece(turn, part):
        return pl.ds(0, levels) if turn == 0 else pl.ds(part * part_rows, part_rows)

    def row_parts(turn):
        return range(1 if turn == 0 else parts)

    def row_copy(turn, part, source_slot, target_slot, device):
        piece = row_piece(turn, part)
        return pltpu.make_async_remote_copy(
            src_ref=row_send.at[turn, source_slot, piece],
            dst_ref=row_recv.at[turn, target_slot, piece],
            send_sem=row_send_sem.at[turn, source_slot, part],
            recv_sem=row_recv_sem.at[turn, target_slot, part],
            device_id=device,
            device_id_type=pl.DeviceIdType.MESH,
        )

    def north_copy(turn, part):
        return row_copy(turn, part, NORTH, north_slot, north)

    def south_copy(turn, part):
        return row_copy(turn, part, SOUTH, NORTH, south)

    def col_copy(turn, source_slot, target_slot, device):
        return pltpu.make_async_remote_copy(
            src_ref=col_send.at[turn, source_slot],
            dst_ref=col_recv.at[turn, target_slot],
            send_sem=col_send_sem.at[turn, source_slot],
            recv_sem=col_recv_sem.at[turn, target_slot],
            device_id=device,
            device_id_type=pl.DeviceIdType.MESH,
        )

    def col_copies(turn):
        return col_copy(turn, EAST, WEST, east), col_copy(turn, WEST, EAST, west)

    def start_rows(turn, part):
        north_copy(turn, part).start()

        @pl.when(has_south)
        def _():
            south_copy(turn, part).start()

    def start_cols(turn):
        for copy in col_copies(turn):
            copy.start()

    def wait_recv(turn):
        for slot in (EAST, WEST):
            pltpu.make_async_copy(
                col_recv.at[turn, slot], col_recv.at[turn, slot], col_recv_sem.at[turn, slot]
            ).wait()

        def arrived(slot):
            for part in row_parts(turn):
                piece = row_recv.at[turn, slot, row_piece(turn, part)]
                pltpu.make_async_copy(piece, piece, row_recv_sem.at[turn, slot, part]).wait()

        arrived(NORTH)

        @pl.when(has_south)
        def _():
            arrived(SOUTH)

    def wait_sent(turn):
        for copy in col_copies(turn):
            copy.wait_send()
        for part in row_parts(turn):
            north_copy(turn, part).wait_send()

        @pl.when(has_south)
        def _():
            for part in row_parts(turn):
                south_copy(turn, part).wait_send()

    @pl.when(jnp.logical_not(has_south))
    def _():
        for turn in range(3):
            row_recv[turn, SOUTH] = jnp.zeros(row_recv.shape[2:], jnp.float32)

    no_row = jnp.zeros((1, cols), jnp.float32)

    def looped(start, stop, unroll, body, carry):
        if unroll >= stop - start:
            for level in range(start, stop):
                carry = body(level, carry)
            return carry

        def outer(index, carried):
            for step in range(unroll):
                carried = body(start + index * unroll + step, carried)
            return carried

        return lax.fori_loop(0, (stop - start) // unroll, outer, carry)

    def packed(level, tracer, value, to_west, to_east):
        place = 2 * level + tracer
        turned = pltpu.roll(value, place, 1)
        to_west = jnp.where(lane == place, turned, to_west)
        to_east = jnp.where(lane == (place + cols - 1) % cols, turned, to_east)
        return to_west, to_east

    empty = jnp.zeros((rows, cols), jnp.float32)

    load_whole(bottom_hbm, bottom, 0).wait()

    one_row = jnp.ones((1, cols), jnp.float32)

    def flag_of(level):
        flag = jnp.where(level < bottom[...], land[level], 0).astype(jnp.float32)
        wet[level, here] = flag
        return flag

    def factor_level(level, carry):
        above, flag, before = carry
        if level + 1 < levels:
            next_flag = flag_of(level + 1)
            below = diff[level + 1] * (flag * next_flag)
        else:
            next_flag, below = empty, empty
        after = []
        for tracer, ratio in enumerate(RATIOS):
            last_q, last_z = before[tracer]
            up, down = ratio * above, ratio * below
            inverse = 1.0 / (1.0 + up + down - up * last_q)
            q = down * inverse
            z = cot[level, tracer] + last_q * last_z
            big_q[level, tracer] = q
            big_i[level, tracer] = flag * inverse
            z_field[level, tracer] = z
            after.append((q, z))
            x_field[level, tracer, pl.ds(PAD - 1, 1)] = no_row
            x_field[level, tracer, pl.ds(PAD + rows, 1)] = no_row
        wet[level, pl.ds(PAD + rows, 1)] = one_row
        lean_v[level, pl.ds(PAD - 1, 1)] = one_row
        return below, next_flag, tuple(after)

    done = 0
    for part in range(CHUNKS):
        for copy in first[part]:
            copy.wait()
        if part == 0:
            carry = (empty, flag_of(0), ((empty, empty), (empty, empty)))
        stop = levels if part + 1 == CHUNKS else (part + 1) * per_chunk - 1
        carry = looped(done, stop, UNROLL, factor_level, carry)
        done = stop

    def upward(turn):
        def level_up(index, carry):
            level = levels - 1 - index
            after, to_west, to_east = carry
            fields = []
            for tracer in range(2):
                x = (
                    z_field[level, tracer] * big_i[level, tracer]
                    + big_q[level, tracer] * after[tracer]
                )
                x_field[level, tracer, here] = x
                to_west, to_east = packed(level, tracer, x, to_west, to_east)
                row_send[turn, NORTH, pl.ds(2 * level + tracer, 1), :] = x[rows - 1 :]
                row_send[turn, SOUTH, pl.ds(2 * level + tracer, 1), :] = x[:1]
                fields.append(x)
            return tuple(fields), to_west, to_east

        carry = ((empty, empty), empty, empty)
        span = levels // parts
        for part in reversed(range(parts)):
            first_index = (parts - 1 - part) * span
            carry = looped(first_index, first_index + span, span // UP_CUT, level_up, carry)
            start_rows(turn, part)
        _, col_send[turn, WEST], col_send[turn, EAST] = carry
        start_cols(turn)

    load_whole(partner_hbm, partner, 6).wait()
    picks = jnp.where(
        is_top, partner[...] - mirror * cols, lax.broadcasted_iota(jnp.int32, (1, cols), 1)
    )
    picks = jnp.broadcast_to(picks, (2 * levels, cols))

    def received(turn):
        wait_recv(turn)
        count = levels if turn == 0 else 2 * levels
        north_rows[turn, :count] = jnp.take_along_axis(
            row_recv[turn, NORTH, :count], picks[:count], axis=1, mode="promise_in_bounds"
        )
        from_east = pltpu.roll(col_recv[turn, EAST], cols - 1, 1)
        from_west = pltpu.roll(col_recv[turn, WEST], 1, 1)
        return (
            jnp.where(lane_even, from_west, from_east),
            jnp.where(lane_even, from_east, from_west),
        )

    def back(level, tracer=0):
        return (cols - (2 * level + tracer)) % cols

    def interior(level, tracer, weights):
        mid, e, w, n, s = weights
        x = x_field[level, tracer, here]
        return (
            mid * x
            + (e * pltpu.roll(x, cols - 1, 1) + w * pltpu.roll(x, 1, 1))
            + (n * x_field[level, tracer, one_north] + s * x_field[level, tracer, one_south])
        )

    def edge_rows(turn, level, tracer):
        place = pl.ds(2 * level + tracer, 1)
        n = c_north[level, rows - 8 :] * north_rows[turn, place, :]
        s = c_south[level, :8] * row_recv[turn, SOUTH, place, :]
        return jnp.where(low_last, n, 0.0), jnp.where(low_first, s, 0.0)

    pl.semaphore_wait(barrier, jnp.where(has_south, 4, 3))
    upward(1)

    def static_level(level, carry):
        to_west, to_east = carry
        flag = wet[level, here]
        lean_u = flag * (LATERAL_MIX - jnp.minimum(u[level], 0.0))
        lean = flag * (LATERAL_MIX - jnp.minimum(v[level], 0.0))
        lean_v[level, here] = lean
        row_send[0, NORTH, pl.ds(level, 1), :] = lean[rows - 1 :]
        row_send[0, SOUTH, pl.ds(level, 1), :] = flag[:1]
        edges = jnp.where(lane < cols // 2, flag, lean_u)
        return packed(level, 0, edges, to_west, to_east)

    for copies in second:
        for copy in copies:
            copy.wait()
    col_send[0, WEST], col_send[0, EAST] = looped(0, levels, UNROLL, static_level, (empty, empty))
    start_rows(0, 0)
    start_cols(0)

    first_lane = jnp.where(lane_first, 1.0, 0.0)

    def weights_level(level, carry):
        flag, u_here = wet[level, here], u[level]
        lean_u = flag * (LATERAL_MIX - jnp.minimum(u_here, 0.0))
        drift_u = flag * (jnp.maximum(u_here, 0.0) + LATERAL_MIX)
        e = drift_u * jnp.where(lane_last, 0.0, pltpu.roll(flag, cols - 1, 1))
        w = flag * jnp.where(lane_first, 0.0, pltpu.roll(lean_u, 1, 1))
        n = flag * wet[level, one_north] * (jnp.maximum(v[level], 0.0) + LATERAL_MIX)
        s = flag * lean_v[level, one_south]
        both = n + s
        both = jnp.concatenate(
            [
                jnp.where(low_first, n[:8], both[:8]),
                both[8 : rows - 8],
                jnp.where(low_last, s[rows - 8 :], both[rows - 8 :]),
            ],
            axis=0,
        )
        mid = ((1.0 - e) - w) - both
        c_mid[level] = mid
        c_east[level] = e
        c_west[level] = w
        c_north[level] = n
        c_south[level] = s
        c_edge[level] = jnp.where(lane_last, drift_u, first_lane * flag)
        for tracer in range(2):
            z_field[level, tracer] = interior(level, tracer, (mid, e, w, n, s))
        return carry

    looped(0, levels, W_UNROLL, weights_level, 0)

    def with_edges(turn, level, tracer, edges, field):
        turned = pltpu.roll(edges[tracer], back(level, tracer), 1)
        total = field[level, tracer] + c_edge[level] * turned
        at_north, at_south = edge_rows(turn, level, tracer)
        return jnp.concatenate(
            [total[:8] + at_south, total[8 : rows - 8], total[rows - 8 :] + at_north], axis=0
        )

    first_edges = received(1)
    static_edges, _ = received(0)

    def down_level(level, carry):
        edge = c_edge[level] * pltpu.roll(static_edges, back(level), 1)
        c_edge[level] = edge
        fold_row = north_rows[0, pl.ds(level, 1), :]
        cut_n, cut_s = c_north[level, rows - 8 :], c_south[level, :8]
        mid_n = jnp.where(low_last, cut_n * jnp.where(is_top, 1.0, fold_row), 0.0)
        mid_s = jnp.where(low_first, cut_s * row_recv[0, SOUTH, pl.ds(level, 1), :], 0.0)
        whole_n = jnp.where(is_top, wet[level, pl.ds(PAD + rows - 8, 8)], cut_n) * fold_row
        c_north[level, rows - 8 :] = jnp.where(low_last, whole_n, cut_n)
        c_south[level, :8] = jnp.where(low_first, mid_s, cut_s)
        mid = c_mid[level] - edge
        c_mid[level] = jnp.concatenate(
            [mid[:8] - mid_s, mid[8 : rows - 8], mid[rows - 8 :] - mid_n], axis=0
        )
        after = []
        for tracer in range(2):
            last_q, last_z = carry[tracer]
            x = x_field[level, tracer, here]
            place = pl.ds(2 * level + tracer, 1)
            turned = pltpu.roll(first_edges[tracer], back(level, tracer), 1)
            total = (z_field[level, tracer] + last_q * last_z) + edge * (turned - x)
            at_n = jnp.where(low_last, whole_n * north_rows[1, place, :], 0.0) - mid_n * x[rows - 8 :]
            at_s = mid_s * (row_recv[1, SOUTH, place, :] - x[:8])
            z = jnp.concatenate(
                [total[:8] + at_s, total[8 : rows - 8], total[rows - 8 :] + at_n], axis=0
            )
            z_field[level, tracer] = z
            after.append((big_q[level, tracer], z))
        return tuple(after)

    looped(0, levels, UNROLL, down_level, ((empty, empty), (empty, empty)))
    upward(2)

    def interior_level(level, carry):
        weights = c_mid[level], c_east[level], c_west[level], c_north[level], c_south[level]
        for tracer in range(2):
            out[level, tracer] = interior(level, tracer, weights)
        return carry

    looped(0, levels, UNROLL, interior_level, 0)
    last_edges = received(2)

    def out_level(level, carry):
        for tracer in range(2):
            out[level, tracer] = with_edges(2, level, tracer, last_edges, out)
        return carry

    looped(0, levels, UNROLL, out_level, 0)
    for turn in range(3):
        wait_sent(turn)


def per_device(cotangent, u_transport, v_transport, diffusivity, land_sea, bottom_level, partner):
    levels, rows, cols = u_transport.shape
    level_field = pltpu.VMEM((levels, rows, cols), jnp.float32)
    pair_field = pltpu.VMEM((levels, 2, rows, cols), jnp.float32)
    anywhere = pl.BlockSpec(memory_space=pl.ANY)
    return pl.pallas_call(
        kernel_body,
        out_shape=pltpu.VMEM(cotangent.shape, jnp.float32),
        in_specs=[anywhere] * 7,
        out_specs=pl.BlockSpec(memory_space=pltpu.VMEM),
        scratch_shapes=[
            pair_field,
            level_field,
            level_field,
            level_field,
            pltpu.VMEM((levels, rows, cols), jnp.int32),
            pltpu.VMEM((rows, cols), jnp.int32),
            pltpu.VMEM((1, cols), jnp.int32),
            pltpu.VMEM((levels, rows + 2 * PAD, cols), jnp.float32),
            pltpu.VMEM((levels, rows + 2 * PAD, cols), jnp.float32),
            pair_field,
            pair_field,
            pltpu.VMEM((levels, 2, rows + 2 * PAD, cols), jnp.float32),
            pair_field,
            level_field,
            level_field,
            level_field,
            level_field,
            level_field,
            level_field,
            pltpu.VMEM((3, 2, 2 * levels, cols), jnp.float32),
            pltpu.VMEM((3, 2, 2 * levels, cols), jnp.float32),
            pltpu.VMEM((3, 2, rows, cols), jnp.float32),
            pltpu.VMEM((3, 2, rows, cols), jnp.float32),
            pltpu.VMEM((3, 2 * levels, cols), jnp.float32),
            pltpu.SemaphoreType.DMA((7, CHUNKS)),
            pltpu.SemaphoreType.DMA((3, 2, ROW_PARTS)),
            pltpu.SemaphoreType.DMA((3, 2, ROW_PARTS)),
            pltpu.SemaphoreType.DMA((3, 2)),
            pltpu.SemaphoreType.DMA((3, 2)),
        ],
        compiler_params=pltpu.CompilerParams(
            collective_id=0, has_side_effects=True, vmem_limit_bytes=30 << 20
        ),
    )(
        *(
            pltpu.with_memory_space_constraint(array, pltpu.HBM)
            for array in (
                cotangent,
                u_transport,
                v_transport,
                diffusivity,
                land_sea,
                bottom_level,
                partner[None, :],
            )
        )
    )


def solution(mesh):
    placed = (
        P(None, None, "lat", "lon"),
        P(None, "lat", "lon"),
        P(None, "lat", "lon"),
        P(None, "lat", "lon"),
        P(None, "lat", "lon"),
        P("lat", "lon"),
        P("lon"),
    )
    return jax.shard_map(
        per_device,
        mesh=mesh,
        in_specs=placed,
        out_specs=P(None, None, "lat", "lon"),
        check_vma=False,
    )
```

```python
import functools

import jax
import jax.numpy as jnp
from jax import lax
from jax.experimental import pallas as pl
from jax.experimental.pallas import tpu as pltpu
from jax.sharding import PartitionSpec as P

LATERAL_MIX = 0.15
SALT_RATIO = 0.5
UNROLL = 40
W_UNROLL = 20
UP_CUT = 1
ROW_PARTS = 5
RATIOS = (1.0, SALT_RATIO)
NORTH, SOUTH = range(2)
EAST, WEST = range(2)
CHUNKS = 5
OUT_CHUNKS = 5
PAD = 8


def kernel_body(
    cot_hbm, u_hbm, v_hbm, diff_hbm, land_hbm, bottom_hbm, partner_hbm,
    out, c_edge, c_north, c_south, out_edges, out_rows,
    cot, u, v, diff, land, bottom, partner, wet, lean_v, big_q, big_i, x_field, z_field,
    c_mid, c_east, c_west,
    row_send, row_recv, col_send, col_recv, north_rows,
    in_sem, row_send_sem, row_recv_sem, col_send_sem, col_recv_sem,
):
    levels, rows, cols = u.shape
    per_chunk = levels // CHUNKS
    lat, lon = lax.axis_index("lat"), lax.axis_index("lon")
    lats, lons = lax.axis_size("lat"), lax.axis_size("lon")
    is_top = lat == lats - 1
    has_south = lat > 0
    mirror = lons - 1 - lon
    east = (lat, lax.rem(lon + 1, lons))
    west = (lat, lax.rem(lon + lons - 1, lons))
    north = (jnp.where(is_top, lat, lat + 1), jnp.where(is_top, mirror, lon))
    south = (jnp.maximum(lat - 1, 0), lon)
    north_slot = jnp.where(is_top, NORTH, SOUTH)

    def signal(device):
        pl.semaphore_signal(
            barrier, inc=1, device_id=device, device_id_type=pl.DeviceIdType.MESH
        )

    barrier = pltpu.get_barrier_semaphore()
    signal(east)
    signal(west)
    signal(north)

    @pl.when(has_south)
    def _():
        signal(south)

    def load_whole(source, target, index):
        return pltpu.make_async_copy(source, target, in_sem.at[index, 0])

    def load_part(source, target, index, part):
        piece = pl.ds(part * per_chunk, per_chunk)
        return pltpu.make_async_copy(source.at[piece], target.at[piece], in_sem.at[index, part])

    whole = [load_whole(bottom_hbm, bottom, 0), load_whole(partner_hbm, partner, 6)]
    first = [
        [load_part(s, t, i, part) for s, t, i in ((land_hbm, land, 1), (diff_hbm, diff, 4), (cot_hbm, cot, 5))]
        for part in range(CHUNKS)
    ]
    second = [
        [load_part(s, t, i, part) for s, t, i in ((u_hbm, u, 2), (v_hbm, v, 3))]
        for part in range(CHUNKS)
    ]
    for copies in [whole] + first + second:
        for copy in copies:
            copy.start()

    lane = lax.broadcasted_iota(jnp.int32, (rows, cols), 1)
    row = lax.broadcasted_iota(jnp.int32, (rows, cols), 0)
    row_last = row == rows - 1
    lane_first, lane_last = lane == 0, lane == cols - 1
    lane_even = lax.rem(lane, 2) == 0
    zero = jnp.minimum(lat, 0)
    here = pl.ds(PAD, rows)
    one_north = pl.ds(PAD + 1 + zero, rows)
    one_south = pl.ds(PAD - 1 + zero, rows)
    row_low = lax.broadcasted_iota(jnp.int32, (8, cols), 0)
    low_first, low_last = row_low == 0, row_low == 7

    parts = row_send_sem.shape[2]
    part_rows = 2 * levels // parts

    def row_piece(turn, part):
        return pl.ds(0, levels) if turn == 0 else pl.ds(part * part_rows, part_rows)

    def row_parts(turn):
        return range(1 if turn == 0 else parts)

    def row_copy(turn, part, source_slot, target_slot, device):
        piece = row_piece(turn, part)
        return pltpu.make_async_remote_copy(
            src_ref=row_send.at[turn, source_slot, piece],
            dst_ref=row_recv.at[turn, target_slot, piece],
            send_sem=row_send_sem.at[turn, source_slot, part],
            recv_sem=row_recv_sem.at[turn, target_slot, part],
            device_id=device,
            device_id_type=pl.DeviceIdType.MESH,
        )

    def north_copy(turn, part):
        return row_copy(turn, part, NORTH, north_slot, north)

    def south_copy(turn, part):
        return row_copy(turn, part, SOUTH, NORTH, south)

    def col_copy(turn, source_slot, target_slot, device):
        return pltpu.make_async_remote_copy(
            src_ref=col_send.at[turn, source_slot],
            dst_ref=col_recv.at[turn, target_slot],
            send_sem=col_send_sem.at[turn, source_slot],
            recv_sem=col_recv_sem.at[turn, target_slot],
            device_id=device,
            device_id_type=pl.DeviceIdType.MESH,
        )

    def col_copies(turn):
        return col_copy(turn, EAST, WEST, east), col_copy(turn, WEST, EAST, west)

    def start_rows(turn, part):
        north_copy(turn, part).start()

        @pl.when(has_south)
        def _():
            south_copy(turn, part).start()

    def start_cols(turn):
        for copy in col_copies(turn):
            copy.start()

    def wait_recv(turn):
        for slot in (EAST, WEST):
            pltpu.make_async_copy(
                col_recv.at[turn, slot], col_recv.at[turn, slot], col_recv_sem.at[turn, slot]
            ).wait()

        def arrived(slot):
            for part in row_parts(turn):
                piece = row_recv.at[turn, slot, row_piece(turn, part)]
                pltpu.make_async_copy(piece, piece, row_recv_sem.at[turn, slot, part]).wait()

        arrived(NORTH)

        @pl.when(has_south)
        def _():
            arrived(SOUTH)

    def wait_sent(turn):
        for copy in col_copies(turn):
            copy.wait_send()
        for part in row_parts(turn):
            north_copy(turn, part).wait_send()

        @pl.when(has_south)
        def _():
            for part in row_parts(turn):
                south_copy(turn, part).wait_send()

    @pl.when(jnp.logical_not(has_south))
    def _():
        for turn in range(3):
            row_recv[turn, SOUTH] = jnp.zeros(row_recv.shape[2:], jnp.float32)

    no_row = jnp.zeros((1, cols), jnp.float32)

    def looped(start, stop, unroll, body, carry):
        if unroll >= stop - start:
            for level in range(start, stop):
                carry = body(level, carry)
            return carry

        def outer(index, carried):
            for step in range(unroll):
                carried = body(start + index * unroll + step, carried)
            return carried

        return lax.fori_loop(0, (stop - start) // unroll, outer, carry)

    def packed(level, tracer, value, to_west, to_east):
        place = 2 * level + tracer
        turned = pltpu.roll(value, place, 1)
        to_west = jnp.where(lane == place, turned, to_west)
        to_east = jnp.where(lane == (place + cols - 1) % cols, turned, to_east)
        return to_west, to_east

    empty = jnp.zeros((rows, cols), jnp.float32)

    load_whole(bottom_hbm, bottom, 0).wait()

    one_row = jnp.ones((1, cols), jnp.float32)

    def flag_of(level):
        flag = jnp.where(level < bottom[...], land[level], 0).astype(jnp.float32)
        wet[level, here] = flag
        return flag

    def factor_level(level, carry):
        above, flag, before = carry
        if level + 1 < levels:
            next_flag = flag_of(level + 1)
            below = diff[level + 1] * (flag * next_flag)
        else:
            next_flag, below = empty, empty
        after = []
        for tracer, ratio in enumerate(RATIOS):
            last_q, last_z = before[tracer]
            up, down = ratio * above, ratio * below
            inverse = 1.0 / (1.0 + up + down - up * last_q)
            q = down * inverse
            z = cot[level, tracer] + last_q * last_z
            big_q[level, tracer] = q
            big_i[level, tracer] = flag * inverse
            z_field[level, tracer] = z
            after.append((q, z))
            x_field[level, tracer, pl.ds(PAD - 1, 1)] = no_row
            x_field[level, tracer, pl.ds(PAD + rows, 1)] = no_row
        wet[level, pl.ds(PAD + rows, 1)] = one_row
        lean_v[level, pl.ds(PAD - 1, 1)] = one_row
        return below, next_flag, tuple(after)

    done = 0
    for part in range(CHUNKS):
        for copy in first[part]:
            copy.wait()
        if part == 0:
            carry = (empty, flag_of(0), ((empty, empty), (empty, empty)))
        stop = levels if part + 1 == CHUNKS else (part + 1) * per_chunk - 1
        carry = looped(done, stop, UNROLL, factor_level, carry)
        done = stop

    def upward(turn):
        def level_up(index, carry):
            level = levels - 1 - index
            after, to_west, to_east = carry
            fields = []
            for tracer in range(2):
                x = (
                    z_field[level, tracer] * big_i[level, tracer]
                    + big_q[level, tracer] * after[tracer]
                )
                x_field[level, tracer, here] = x
                to_west, to_east = packed(level, tracer, x, to_west, to_east)
                row_send[turn, NORTH, pl.ds(2 * level + tracer, 1), :] = x[rows - 1 :]
                row_send[turn, SOUTH, pl.ds(2 * level + tracer, 1), :] = x[:1]
                fields.append(x)
            return tuple(fields), to_west, to_east

        carry = ((empty, empty), empty, empty)
        span = levels // parts
        for part in reversed(range(parts)):
            first_index = (parts - 1 - part) * span
            carry = looped(first_index, first_index + span, span // UP_CUT, level_up, carry)
            start_rows(turn, part)
        _, col_send[turn, WEST], col_send[turn, EAST] = carry
        start_cols(turn)

    load_whole(partner_hbm, partner, 6).wait()
    picks = jnp.where(
        is_top, partner[...] - mirror * cols, lax.broadcasted_iota(jnp.int32, (1, cols), 1)
    )
    picks = jnp.broadcast_to(picks, (2 * levels, cols))

    def received(turn):
        wait_recv(turn)
        count = levels if turn == 0 else 2 * levels
        north_rows[turn, :count] = jnp.take_along_axis(
            row_recv[turn, NORTH, :count], picks[:count], axis=1, mode="promise_in_bounds"
        )
        from_east = pltpu.roll(col_recv[turn, EAST], cols - 1, 1)
        from_west = pltpu.roll(col_recv[turn, WEST], 1, 1)
        return (
            jnp.where(lane_even, from_west, from_east),
            jnp.where(lane_even, from_east, from_west),
        )

    def back(level, tracer=0):
        return (cols - (2 * level + tracer)) % cols

    def interior(level, tracer, weights):
        mid, e, w, n, s = weights
        x = x_field[level, tracer, here]
        return (
            mid * x
            + (e * pltpu.roll(x, cols - 1, 1) + w * pltpu.roll(x, 1, 1))
            + (n * x_field[level, tracer, one_north] + s * x_field[level, tracer, one_south])
        )

    pl.semaphore_wait(barrier, jnp.where(has_south, 4, 3))
    upward(1)

    def static_level(level, carry):
        to_west, to_east = carry
        flag = wet[level, here]
        lean_u = flag * (LATERAL_MIX - jnp.minimum(u[level], 0.0))
        lean = flag * (LATERAL_MIX - jnp.minimum(v[level], 0.0))
        lean_v[level, here] = lean
        row_send[0, NORTH, pl.ds(level, 1), :] = lean[rows - 1 :]
        row_send[0, SOUTH, pl.ds(level, 1), :] = flag[:1]
        edges = jnp.where(lane < cols // 2, flag, lean_u)
        return packed(level, 0, edges, to_west, to_east)

    for copies in second:
        for copy in copies:
            copy.wait()
    col_send[0, WEST], col_send[0, EAST] = looped(0, levels, UNROLL, static_level, (empty, empty))
    start_rows(0, 0)
    start_cols(0)

    first_lane = jnp.where(lane_first, 1.0, 0.0)

    def weights_level(level, carry):
        flag, u_here = wet[level, here], u[level]
        lean_u = flag * (LATERAL_MIX - jnp.minimum(u_here, 0.0))
        drift_u = flag * (jnp.maximum(u_here, 0.0) + LATERAL_MIX)
        e = drift_u * jnp.where(lane_last, 0.0, pltpu.roll(flag, cols - 1, 1))
        w = flag * jnp.where(lane_first, 0.0, pltpu.roll(lean_u, 1, 1))
        n = flag * wet[level, one_north] * (jnp.maximum(v[level], 0.0) + LATERAL_MIX)
        s = flag * lean_v[level, one_south]
        both = n + s
        both = jnp.concatenate(
            [
                jnp.where(low_first, n[:8], both[:8]),
                both[8 : rows - 8],
                jnp.where(low_last, s[rows - 8 :], both[rows - 8 :]),
            ],
            axis=0,
        )
        mid = ((1.0 - e) - w) - both
        c_mid[level] = mid
        c_east[level] = e
        c_west[level] = w
        c_north[level] = n
        c_south[level] = s
        c_edge[level] = jnp.where(lane_last, drift_u, first_lane * flag)
        for tracer in range(2):
            z_field[level, tracer] = interior(level, tracer, (mid, e, w, n, s))
        return carry

    looped(0, levels, W_UNROLL, weights_level, 0)

    first_edges = received(1)
    static_edges, _ = received(0)

    def down_level(level, carry):
        edge = c_edge[level] * pltpu.roll(static_edges, back(level), 1)
        c_edge[level] = edge
        fold_row = north_rows[0, pl.ds(level, 1), :]
        cut_n, cut_s = c_north[level, rows - 8 :], c_south[level, :8]
        mid_n = jnp.where(low_last, cut_n * jnp.where(is_top, 1.0, fold_row), 0.0)
        mid_s = jnp.where(low_first, cut_s * row_recv[0, SOUTH, pl.ds(level, 1), :], 0.0)
        whole_n = jnp.where(is_top, wet[level, pl.ds(PAD + rows - 8, 8)], cut_n) * fold_row
        c_north[level, rows - 8 :] = jnp.where(low_last, whole_n, cut_n)
        c_south[level, :8] = jnp.where(low_first, mid_s, cut_s)
        mid = c_mid[level] - edge
        c_mid[level] = jnp.concatenate(
            [mid[:8] - mid_s, mid[8 : rows - 8], mid[rows - 8 :] - mid_n], axis=0
        )
        after = []
        for tracer in range(2):
            last_q, last_z = carry[tracer]
            x = x_field[level, tracer, here]
            place = pl.ds(2 * level + tracer, 1)
            turned = pltpu.roll(first_edges[tracer], back(level, tracer), 1)
            total = (z_field[level, tracer] + last_q * last_z) + edge * (turned - x)
            at_n = jnp.where(low_last, whole_n * north_rows[1, place, :], 0.0) - mid_n * x[rows - 8 :]
            at_s = mid_s * (row_recv[1, SOUTH, place, :] - x[:8])
            z = jnp.concatenate(
                [total[:8] + at_s, total[8 : rows - 8], total[rows - 8 :] + at_n], axis=0
            )
            z_field[level, tracer] = z
            after.append((big_q[level, tracer], z))
        return tuple(after)

    looped(0, levels, UNROLL, down_level, ((empty, empty), (empty, empty)))
    upward(2)

    def interior_level(level, carry):
        weights = c_mid[level], c_east[level], c_west[level], c_north[level], c_south[level]
        for tracer in range(2):
            out[level, tracer] = interior(level, tracer, weights)
        return carry

    looped(0, levels, UNROLL, interior_level, 0)
    out_edges[0], out_edges[1] = received(2)
    out_rows[NORTH] = north_rows[2]
    out_rows[SOUTH] = row_recv[2, SOUTH]
    for turn in range(3):
        wait_sent(turn)


def finish_body(part, c_edge, c_north, c_south, edges, rows_in, out_hbm, out, out_sem):
    levels, _, rows, cols = part.shape
    row_low = lax.broadcasted_iota(jnp.int32, (8, cols), 0)
    low_first, low_last = row_low == 0, row_low == 7
    per_chunk = levels // OUT_CHUNKS

    def copy(chunk):
        piece = pl.ds(chunk * per_chunk, per_chunk)
        return pltpu.make_async_copy(out.at[piece], out_hbm.at[piece], out_sem.at[chunk])

    for level in range(levels):
        for tracer in range(2):
            place = 2 * level + tracer
            turned = pltpu.roll(edges[tracer], (cols - place) % cols, 1)
            total = part[level, tracer] + c_edge[level] * turned
            n = c_north[level, rows - 8 :] * rows_in[NORTH, pl.ds(place, 1), :]
            s = c_south[level, :8] * rows_in[SOUTH, pl.ds(place, 1), :]
            out[level, tracer, :8] = total[:8] + jnp.where(low_first, s, 0.0)
            out[level, tracer, 8 : rows - 8] = total[8 : rows - 8]
            out[level, tracer, rows - 8 :] = total[rows - 8 :] + jnp.where(low_last, n, 0.0)
        if (level + 1) % per_chunk == 0:
            copy(level // per_chunk).start()
    for chunk in range(OUT_CHUNKS):
        copy(chunk).wait()


def per_device(cotangent, u_transport, v_transport, diffusivity, land_sea, bottom_level, partner):
    levels, rows, cols = u_transport.shape
    level_field = pltpu.VMEM((levels, rows, cols), jnp.float32)
    pair_field = pltpu.VMEM((levels, 2, rows, cols), jnp.float32)
    anywhere = pl.BlockSpec(memory_space=pl.ANY)
    whole = pl.BlockSpec(memory_space=pltpu.VMEM)
    parts = pl.pallas_call(
        kernel_body,
        out_shape=[
            pair_field,
            level_field,
            level_field,
            level_field,
            pltpu.VMEM((2, rows, cols), jnp.float32),
            pltpu.VMEM((2, 2 * levels, cols), jnp.float32),
        ],
        in_specs=[anywhere] * 7,
        out_specs=[whole] * 6,
        scratch_shapes=[
            pair_field,
            level_field,
            level_field,
            level_field,
            pltpu.VMEM((levels, rows, cols), jnp.int32),
            pltpu.VMEM((rows, cols), jnp.int32),
            pltpu.VMEM((1, cols), jnp.int32),
            pltpu.VMEM((levels, rows + 2 * PAD, cols), jnp.float32),
            pltpu.VMEM((levels, rows + 2 * PAD, cols), jnp.float32),
            pair_field,
            pair_field,
            pltpu.VMEM((levels, 2, rows + 2 * PAD, cols), jnp.float32),
            pair_field,
            level_field,
            level_field,
            level_field,
            pltpu.VMEM((3, 2, 2 * levels, cols), jnp.float32),
            pltpu.VMEM((3, 2, 2 * levels, cols), jnp.float32),
            pltpu.VMEM((3, 2, rows, cols), jnp.float32),
            pltpu.VMEM((3, 2, rows, cols), jnp.float32),
            pltpu.VMEM((3, 2 * levels, cols), jnp.float32),
            pltpu.SemaphoreType.DMA((7, CHUNKS)),
            pltpu.SemaphoreType.DMA((3, 2, ROW_PARTS)),
            pltpu.SemaphoreType.DMA((3, 2, ROW_PARTS)),
            pltpu.SemaphoreType.DMA((3, 2)),
            pltpu.SemaphoreType.DMA((3, 2)),
        ],
        compiler_params=pltpu.CompilerParams(
            collective_id=0, has_side_effects=True, vmem_limit_bytes=30 << 20
        ),
    )(
        *(
            pltpu.with_memory_space_constraint(array, pltpu.HBM)
            for array in (
                cotangent,
                u_transport,
                v_transport,
                diffusivity,
                land_sea,
                bottom_level,
                partner[None, :],
            )
        )
    )
    return pl.pallas_call(
        finish_body,
        out_shape=jax.ShapeDtypeStruct(cotangent.shape, jnp.float32),
        in_specs=[whole] * 6,
        out_specs=anywhere,
        scratch_shapes=[pair_field, pltpu.SemaphoreType.DMA((OUT_CHUNKS,))],
        compiler_params=pltpu.CompilerParams(vmem_limit_bytes=30 << 20),
    )(*parts)


def solution(mesh):
    placed = (
        P(None, None, "lat", "lon"),
        P(None, "lat", "lon"),
        P(None, "lat", "lon"),
        P(None, "lat", "lon"),
        P(None, "lat", "lon"),
        P("lat", "lon"),
        P("lon"),
    )
    return jax.shard_map(
        per_device,
        mesh=mesh,
        in_specs=placed,
        out_specs=P(None, None, "lat", "lon"),
        check_vma=False,
    )
```

```python
import functools

import jax
import jax.numpy as jnp
from jax import lax
from jax.experimental import pallas as pl
from jax.experimental.pallas import tpu as pltpu
from jax.sharding import PartitionSpec as P

LATERAL_MIX = 0.15
SALT_RATIO = 0.5
UNROLL = 40
W_UNROLL = 20
UP_CUT = 1
ROW_PARTS = 2
RATIOS = (1.0, SALT_RATIO)
NORTH, SOUTH = range(2)
EAST, WEST = range(2)
CHUNKS = 5
OUT_CHUNKS = 5
PAD = 8


def kernel_body(
    cot_hbm, u_hbm, v_hbm, diff_hbm, land_hbm, bottom_hbm, partner_hbm,
    out, c_edge, c_north, c_south, out_edges, out_rows,
    cot, u, v, diff, land, bottom, partner, wet, lean_v, big_q, big_i, x_field, z_field,
    c_mid, c_east, c_west,
    row_send, row_recv, col_send, col_recv, north_rows,
    in_sem, row_send_sem, row_recv_sem, col_send_sem, col_recv_sem,
):
    levels, rows, cols = u.shape
    per_chunk = levels // CHUNKS
    lat, lon = lax.axis_index("lat"), lax.axis_index("lon")
    lats, lons = lax.axis_size("lat"), lax.axis_size("lon")
    is_top = lat == lats - 1
    has_south = lat > 0
    mirror = lons - 1 - lon
    east = (lat, lax.rem(lon + 1, lons))
    west = (lat, lax.rem(lon + lons - 1, lons))
    north = (jnp.where(is_top, lat, lat + 1), jnp.where(is_top, mirror, lon))
    south = (jnp.maximum(lat - 1, 0), lon)
    north_slot = jnp.where(is_top, NORTH, SOUTH)

    def signal(device):
        pl.semaphore_signal(
            barrier, inc=1, device_id=device, device_id_type=pl.DeviceIdType.MESH
        )

    barrier = pltpu.get_barrier_semaphore()
    signal(east)
    signal(west)
    signal(north)

    @pl.when(has_south)
    def _():
        signal(south)

    def load_whole(source, target, index):
        return pltpu.make_async_copy(source, target, in_sem.at[index, 0])

    def load_part(source, target, index, part):
        piece = pl.ds(part * per_chunk, per_chunk)
        return pltpu.make_async_copy(source.at[piece], target.at[piece], in_sem.at[index, part])

    whole = [load_whole(bottom_hbm, bottom, 0), load_whole(partner_hbm, partner, 6)]
    first = [
        [load_part(s, t, i, part) for s, t, i in ((land_hbm, land, 1), (diff_hbm, diff, 4), (cot_hbm, cot, 5))]
        for part in range(CHUNKS)
    ]
    second = [
        [load_part(s, t, i, part) for s, t, i in ((u_hbm, u, 2), (v_hbm, v, 3))]
        for part in range(CHUNKS)
    ]
    for copies in [whole] + first + second:
        for copy in copies:
            copy.start()

    lane = lax.broadcasted_iota(jnp.int32, (rows, cols), 1)
    row = lax.broadcasted_iota(jnp.int32, (rows, cols), 0)
    row_last = row == rows - 1
    lane_first, lane_last = lane == 0, lane == cols - 1
    lane_even = lax.rem(lane, 2) == 0
    lane_slot = lax.rem(lane + 1, cols) // 2
    zero = jnp.minimum(lat, 0)
    here = pl.ds(PAD, rows)
    one_north = pl.ds(PAD + 1 + zero, rows)
    one_south = pl.ds(PAD - 1 + zero, rows)
    row_low = lax.broadcasted_iota(jnp.int32, (8, cols), 0)
    low_first, low_last = row_low == 0, row_low == 7

    parts = row_send_sem.shape[2]
    part_rows = 2 * levels // parts

    def row_piece(turn, part):
        return pl.ds(0, levels) if turn == 0 else pl.ds(part * part_rows, part_rows)

    def row_parts(turn):
        return range(1 if turn == 0 else parts)

    def row_copy(turn, part, source_slot, target_slot, device):
        piece = row_piece(turn, part)
        return pltpu.make_async_remote_copy(
            src_ref=row_send.at[turn, source_slot, piece],
            dst_ref=row_recv.at[turn, target_slot, piece],
            send_sem=row_send_sem.at[turn, source_slot, part],
            recv_sem=row_recv_sem.at[turn, target_slot, part],
            device_id=device,
            device_id_type=pl.DeviceIdType.MESH,
        )

    def north_copy(turn, part):
        return row_copy(turn, part, NORTH, north_slot, north)

    def south_copy(turn, part):
        return row_copy(turn, part, SOUTH, NORTH, south)

    def col_copy(turn, source_slot, target_slot, device):
        return pltpu.make_async_remote_copy(
            src_ref=col_send.at[turn, source_slot],
            dst_ref=col_recv.at[turn, target_slot],
            send_sem=col_send_sem.at[turn, source_slot],
            recv_sem=col_recv_sem.at[turn, target_slot],
            device_id=device,
            device_id_type=pl.DeviceIdType.MESH,
        )

    def col_copies(turn):
        return col_copy(turn, EAST, WEST, east), col_copy(turn, WEST, EAST, west)

    def start_rows(turn, part):
        north_copy(turn, part).start()

        @pl.when(has_south)
        def _():
            south_copy(turn, part).start()

    def start_cols(turn):
        for copy in col_copies(turn):
            copy.start()

    def wait_recv(turn):
        for slot in (EAST, WEST):
            pltpu.make_async_copy(
                col_recv.at[turn, slot], col_recv.at[turn, slot], col_recv_sem.at[turn, slot]
            ).wait()

        def arrived(slot):
            for part in row_parts(turn):
                piece = row_recv.at[turn, slot, row_piece(turn, part)]
                pltpu.make_async_copy(piece, piece, row_recv_sem.at[turn, slot, part]).wait()

        arrived(NORTH)

        @pl.when(has_south)
        def _():
            arrived(SOUTH)

    def wait_sent(turn):
        for copy in col_copies(turn):
            copy.wait_send()
        for part in row_parts(turn):
            north_copy(turn, part).wait_send()

        @pl.when(has_south)
        def _():
            for part in row_parts(turn):
                south_copy(turn, part).wait_send()

    @pl.when(jnp.logical_not(has_south))
    def _():
        for turn in range(3):
            row_recv[turn, SOUTH] = jnp.zeros(row_recv.shape[2:], jnp.float32)

    no_row = jnp.zeros((1, cols), jnp.float32)

    def looped(start, stop, unroll, body, carry):
        if unroll >= stop - start:
            for level in range(start, stop):
                carry = body(level, carry)
            return carry

        def outer(index, carried):
            for step in range(unroll):
                carried = body(start + index * unroll + step, carried)
            return carried

        return lax.fori_loop(0, (stop - start) // unroll, outer, carry)

    def packed(level, tracer, value, to_west, to_east):
        place = 2 * level + tracer
        turned = pltpu.roll(value, place, 1)
        to_west = jnp.where(lane == place, turned, to_west)
        to_east = jnp.where(lane == (place + cols - 1) % cols, turned, to_east)
        return to_west, to_east

    def gathered(level, value, kept):
        return jnp.where(lane_slot == level, pltpu.roll(value, 2 * level, 1), kept)

    def parted(first_kept, second_kept):
        moved = pltpu.roll(second_kept, 1, 1)
        return jnp.where(lane_even, first_kept, moved), jnp.where(lane_even, moved, first_kept)

    empty = jnp.zeros((rows, cols), jnp.float32)

    load_whole(bottom_hbm, bottom, 0).wait()

    one_row = jnp.ones((1, cols), jnp.float32)

    def flag_of(level):
        flag = jnp.where(level < bottom[...], land[level], 0).astype(jnp.float32)
        wet[level, here] = flag
        return flag

    def factor_level(level, carry):
        above, flag, before = carry
        if level + 1 < levels:
            next_flag = flag_of(level + 1)
            below = diff[level + 1] * (flag * next_flag)
        else:
            next_flag, below = empty, empty
        after = []
        for tracer, ratio in enumerate(RATIOS):
            last_q, last_z = before[tracer]
            up, down = ratio * above, ratio * below
            inverse = 1.0 / (1.0 + up + down - up * last_q)
            q = down * inverse
            z = cot[level, tracer] + last_q * last_z
            big_q[level, tracer] = q
            big_i[level, tracer] = flag * inverse
            z_field[level, tracer] = z
            after.append((q, z))
            x_field[level, tracer, pl.ds(PAD - 1, 1)] = no_row
            x_field[level, tracer, pl.ds(PAD + rows, 1)] = no_row
        wet[level, pl.ds(PAD + rows, 1)] = one_row
        lean_v[level, pl.ds(PAD - 1, 1)] = one_row
        return below, next_flag, tuple(after)

    done = 0
    for part in range(CHUNKS):
        for copy in first[part]:
            copy.wait()
        if part == 0:
            carry = (empty, flag_of(0), ((empty, empty), (empty, empty)))
        stop = levels if part + 1 == CHUNKS else (part + 1) * per_chunk - 1
        carry = looped(done, stop, UNROLL, factor_level, carry)
        done = stop

    def upward(turn):
        def level_up(index, carry):
            level = levels - 1 - index
            after, kept = carry
            fields, edges = [], []
            for tracer in range(2):
                x = (
                    z_field[level, tracer] * big_i[level, tracer]
                    + big_q[level, tracer] * after[tracer]
                )
                x_field[level, tracer, here] = x
                edges.append(gathered(level, x, kept[tracer]))
                row_send[turn, NORTH, pl.ds(2 * level + tracer, 1), :] = x[rows - 1 :]
                row_send[turn, SOUTH, pl.ds(2 * level + tracer, 1), :] = x[:1]
                fields.append(x)
            return tuple(fields), tuple(edges)

        carry = ((empty, empty), (empty, empty))
        span = levels // parts
        for part in reversed(range(parts)):
            first_index = (parts - 1 - part) * span
            carry = looped(first_index, first_index + span, span // UP_CUT, level_up, carry)
            start_rows(turn, part)
        col_send[turn, WEST], col_send[turn, EAST] = parted(*carry[1])
        start_cols(turn)

    load_whole(partner_hbm, partner, 6).wait()
    picks = jnp.where(
        is_top, partner[...] - mirror * cols, lax.broadcasted_iota(jnp.int32, (1, cols), 1)
    )
    picks = jnp.broadcast_to(picks, (2 * levels, cols))

    def received(turn):
        wait_recv(turn)
        count = levels if turn == 0 else 2 * levels
        north_rows[turn, :count] = jnp.take_along_axis(
            row_recv[turn, NORTH, :count], picks[:count], axis=1, mode="promise_in_bounds"
        )
        from_east = pltpu.roll(col_recv[turn, EAST], cols - 1, 1)
        from_west = pltpu.roll(col_recv[turn, WEST], 1, 1)
        return (
            jnp.where(lane_even, from_west, from_east),
            jnp.where(lane_even, from_east, from_west),
        )

    def back(level, tracer=0):
        return (cols - (2 * level + tracer)) % cols

    def interior(level, tracer, weights):
        mid, e, w, n, s = weights
        x = x_field[level, tracer, here]
        return (
            mid * x
            + (e * pltpu.roll(x, cols - 1, 1) + w * pltpu.roll(x, 1, 1))
            + (n * x_field[level, tracer, one_north] + s * x_field[level, tracer, one_south])
        )

    pl.semaphore_wait(barrier, jnp.where(has_south, 4, 3))
    upward(1)

    def static_level(level, carry):
        to_west, to_east = carry
        flag = wet[level, here]
        lean_u = flag * (LATERAL_MIX - jnp.minimum(u[level], 0.0))
        lean = flag * (LATERAL_MIX - jnp.minimum(v[level], 0.0))
        lean_v[level, here] = lean
        row_send[0, NORTH, pl.ds(level, 1), :] = lean[rows - 1 :]
        row_send[0, SOUTH, pl.ds(level, 1), :] = flag[:1]
        edges = jnp.where(lane < cols // 2, flag, lean_u)
        return packed(level, 0, edges, to_west, to_east)

    for copies in second:
        for copy in copies:
            copy.wait()
    col_send[0, WEST], col_send[0, EAST] = looped(0, levels, UNROLL, static_level, (empty, empty))
    start_rows(0, 0)
    start_cols(0)

    first_lane = jnp.where(lane_first, 1.0, 0.0)

    def weights_level(level, carry):
        flag, u_here = wet[level, here], u[level]
        lean_u = flag * (LATERAL_MIX - jnp.minimum(u_here, 0.0))
        drift_u = flag * (jnp.maximum(u_here, 0.0) + LATERAL_MIX)
        e = drift_u * jnp.where(lane_last, 0.0, pltpu.roll(flag, cols - 1, 1))
        w = flag * jnp.where(lane_first, 0.0, pltpu.roll(lean_u, 1, 1))
        n = flag * wet[level, one_north] * (jnp.maximum(v[level], 0.0) + LATERAL_MIX)
        s = flag * lean_v[level, one_south]
        both = n + s
        both = jnp.concatenate(
            [
                jnp.where(low_first, n[:8], both[:8]),
                both[8 : rows - 8],
                jnp.where(low_last, s[rows - 8 :], both[rows - 8 :]),
            ],
            axis=0,
        )
        mid = ((1.0 - e) - w) - both
        c_mid[level] = mid
        c_east[level] = e
        c_west[level] = w
        c_north[level] = n
        c_south[level] = s
        c_edge[level] = jnp.where(lane_last, drift_u, first_lane * flag)
        for tracer in range(2):
            z_field[level, tracer] = interior(level, tracer, (mid, e, w, n, s))
        return carry

    looped(0, levels, W_UNROLL, weights_level, 0)

    first_edges = received(1)
    static_edges, _ = received(0)
    own_west, own_east = col_send[1, WEST], col_send[1, EAST]
    first_edges = (
        static_edges * (first_edges[0] - jnp.where(lane_even, own_west, own_east)),
        pltpu.roll(static_edges, 1, 1)
        * (first_edges[1] - jnp.where(lane_even, own_east, own_west)),
    )

    def row_weights(level):
        fold_row = north_rows[0, pl.ds(level, 1), :]
        cut_n, cut_s = c_north[level, rows - 8 :], c_south[level, :8]
        mid_n = jnp.where(low_last, cut_n * jnp.where(is_top, 1.0, fold_row), 0.0)
        mid_s = jnp.where(low_first, cut_s * row_recv[0, SOUTH, pl.ds(level, 1), :], 0.0)
        whole_n = jnp.where(is_top, wet[level, pl.ds(PAD + rows - 8, 8)], cut_n) * fold_row
        return cut_n, cut_s, mid_n, mid_s, whole_n

    def down_level(level, carry):
        _, _, mid_n, mid_s, whole_n = row_weights(level)
        edge = c_edge[level]
        after = []
        for tracer in range(2):
            last_q, last_z = carry[tracer]
            place = pl.ds(2 * level + tracer, 1)
            turned = pltpu.roll(first_edges[tracer], back(level, tracer), 1)
            total = (z_field[level, tracer] + last_q * last_z) + edge * turned
            x_n = x_field[level, tracer, pl.ds(PAD + rows - 8, 8)]
            x_s = x_field[level, tracer, pl.ds(PAD, 8)]
            at_n = jnp.where(low_last, whole_n * north_rows[1, place, :], 0.0) - mid_n * x_n
            at_s = mid_s * (row_recv[1, SOUTH, place, :] - x_s)
            z = jnp.concatenate(
                [total[:8] + at_s, total[8 : rows - 8], total[rows - 8 :] + at_n], axis=0
            )
            z_field[level, tracer] = z
            after.append((big_q[level, tracer], z))
        return tuple(after)

    looped(0, levels, UNROLL, down_level, ((empty, empty), (empty, empty)))
    upward(2)

    def interior_level(level, carry):
        cut_n, cut_s, mid_n, mid_s, whole_n = row_weights(level)
        edge = c_edge[level] * pltpu.roll(static_edges, back(level), 1)
        c_edge[level] = edge
        mid = c_mid[level] - edge
        mid = jnp.concatenate(
            [mid[:8] - mid_s, mid[8 : rows - 8], mid[rows - 8 :] - mid_n], axis=0
        )
        weights = mid, c_east[level], c_west[level], c_north[level], c_south[level]
        c_north[level, rows - 8 :] = jnp.where(low_last, whole_n, cut_n)
        c_south[level, :8] = jnp.where(low_first, mid_s, cut_s)
        for tracer in range(2):
            out[level, tracer] = interior(level, tracer, weights)
        return carry

    looped(0, levels, UNROLL, interior_level, 0)
    out_edges[0], out_edges[1] = received(2)
    out_rows[NORTH] = north_rows[2]
    out_rows[SOUTH] = row_recv[2, SOUTH]
    for turn in range(3):
        wait_sent(turn)


def finish_body(part, c_edge, c_north, c_south, edges, rows_in, out_hbm, out, out_sem):
    levels, _, rows, cols = part.shape
    row_low = lax.broadcasted_iota(jnp.int32, (8, cols), 0)
    low_first, low_last = row_low == 0, row_low == 7
    per_chunk = levels // OUT_CHUNKS

    def copy(chunk):
        piece = pl.ds(chunk * per_chunk, per_chunk)
        return pltpu.make_async_copy(out.at[piece], out_hbm.at[piece], out_sem.at[chunk])

    for level in range(levels):
        for tracer in range(2):
            place = 2 * level + tracer
            turned = pltpu.roll(edges[tracer], (cols - place) % cols, 1)
            total = part[level, tracer] + c_edge[level] * turned
            n = c_north[level, rows - 8 :] * rows_in[NORTH, pl.ds(place, 1), :]
            s = c_south[level, :8] * rows_in[SOUTH, pl.ds(place, 1), :]
            out[level, tracer, :8] = total[:8] + jnp.where(low_first, s, 0.0)
            out[level, tracer, 8 : rows - 8] = total[8 : rows - 8]
            out[level, tracer, rows - 8 :] = total[rows - 8 :] + jnp.where(low_last, n, 0.0)
        if (level + 1) % per_chunk == 0:
            copy(level // per_chunk).start()
    for chunk in range(OUT_CHUNKS):
        copy(chunk).wait()


def per_device(cotangent, u_transport, v_transport, diffusivity, land_sea, bottom_level, partner):
    levels, rows, cols = u_transport.shape
    level_field = pltpu.VMEM((levels, rows, cols), jnp.float32)
    pair_field = pltpu.VMEM((levels, 2, rows, cols), jnp.float32)
    anywhere = pl.BlockSpec(memory_space=pl.ANY)
    whole = pl.BlockSpec(memory_space=pltpu.VMEM)
    parts = pl.pallas_call(
        kernel_body,
        out_shape=[
            pair_field,
            level_field,
            level_field,
            level_field,
            pltpu.VMEM((2, rows, cols), jnp.float32),
            pltpu.VMEM((2, 2 * levels, cols), jnp.float32),
        ],
        in_specs=[anywhere] * 7,
        out_specs=[whole] * 6,
        scratch_shapes=[
            pair_field,
            level_field,
            level_field,
            level_field,
            pltpu.VMEM((levels, rows, cols), jnp.int32),
            pltpu.VMEM((rows, cols), jnp.int32),
            pltpu.VMEM((1, cols), jnp.int32),
            pltpu.VMEM((levels, rows + 2 * PAD, cols), jnp.float32),
            pltpu.VMEM((levels, rows + 2 * PAD, cols), jnp.float32),
            pair_field,
            pair_field,
            pltpu.VMEM((levels, 2, rows + 2 * PAD, cols), jnp.float32),
            pair_field,
            level_field,
            level_field,
            level_field,
            pltpu.VMEM((3, 2, 2 * levels, cols), jnp.float32),
            pltpu.VMEM((3, 2, 2 * levels, cols), jnp.float32),
            pltpu.VMEM((3, 2, rows, cols), jnp.float32),
            pltpu.VMEM((3, 2, rows, cols), jnp.float32),
            pltpu.VMEM((3, 2 * levels, cols), jnp.float32),
            pltpu.SemaphoreType.DMA((7, CHUNKS)),
            pltpu.SemaphoreType.DMA((3, 2, ROW_PARTS)),
            pltpu.SemaphoreType.DMA((3, 2, ROW_PARTS)),
            pltpu.SemaphoreType.DMA((3, 2)),
            pltpu.SemaphoreType.DMA((3, 2)),
        ],
        compiler_params=pltpu.CompilerParams(
            collective_id=0, has_side_effects=True, vmem_limit_bytes=30 << 20
        ),
    )(
        *(
            pltpu.with_memory_space_constraint(array, pltpu.HBM)
            for array in (
                cotangent,
                u_transport,
                v_transport,
                diffusivity,
                land_sea,
                bottom_level,
                partner[None, :],
            )
        )
    )
    return pl.pallas_call(
        finish_body,
        out_shape=jax.ShapeDtypeStruct(cotangent.shape, jnp.float32),
        in_specs=[whole] * 6,
        out_specs=anywhere,
        scratch_shapes=[pair_field, pltpu.SemaphoreType.DMA((OUT_CHUNKS,))],
        compiler_params=pltpu.CompilerParams(vmem_limit_bytes=30 << 20),
    )(*parts)


def solution(mesh):
    placed = (
        P(None, None, "lat", "lon"),
        P(None, "lat", "lon"),
        P(None, "lat", "lon"),
        P(None, "lat", "lon"),
        P(None, "lat", "lon"),
        P("lat", "lon"),
        P("lon"),
    )
    return jax.shard_map(
        per_device,
        mesh=mesh,
        in_specs=placed,
        out_specs=P(None, None, "lat", "lon"),
        check_vma=False,
    )
```

```python
import functools

import jax
import jax.numpy as jnp
from jax import lax
from jax.experimental import pallas as pl
from jax.experimental.pallas import tpu as pltpu
from jax.sharding import PartitionSpec as P

LATERAL_MIX = 0.15
SALT_RATIO = 0.5
UNROLL = 40
W_UNROLL = 20
UP_CUT = 1
ROW_PARTS = 2
RATIOS = (1.0, SALT_RATIO)
NORTH, SOUTH = range(2)
EAST, WEST = range(2)
CHUNKS = 5
OUT_CHUNKS = 5
PAD = 8


def kernel_body(
    cot_hbm, u_hbm, v_hbm, diff_hbm, land_hbm, bottom_hbm, partner_hbm,
    out, c_edge, c_north, c_south, out_edges, out_rows,
    cot, u, v, diff, land, bottom, partner, wet, lean_v, big_q, big_i, x_field, z_field,
    c_mid, c_east, c_west,
    row_send, row_recv, col_send, col_recv, north_rows, v_top,
    in_sem, row_send_sem, row_recv_sem, col_send_sem, col_recv_sem,
):
    levels, rows, cols = u.shape
    per_chunk = levels // CHUNKS
    lat, lon = lax.axis_index("lat"), lax.axis_index("lon")
    lats, lons = lax.axis_size("lat"), lax.axis_size("lon")
    is_top = lat == lats - 1
    has_south = lat > 0
    mirror = lons - 1 - lon
    east = (lat, lax.rem(lon + 1, lons))
    west = (lat, lax.rem(lon + lons - 1, lons))
    north = (jnp.where(is_top, lat, lat + 1), jnp.where(is_top, mirror, lon))
    south = (jnp.maximum(lat - 1, 0), lon)
    north_slot = jnp.where(is_top, NORTH, SOUTH)

    def signal(device):
        pl.semaphore_signal(
            barrier, inc=1, device_id=device, device_id_type=pl.DeviceIdType.MESH
        )

    barrier = pltpu.get_barrier_semaphore()
    signal(east)
    signal(west)
    signal(north)

    @pl.when(has_south)
    def _():
        signal(south)

    def load_whole(source, target, index):
        return pltpu.make_async_copy(source, target, in_sem.at[index, 0])

    def load_part(source, target, index, part):
        piece = pl.ds(part * per_chunk, per_chunk)
        return pltpu.make_async_copy(source.at[piece], target.at[piece], in_sem.at[index, part])

    whole = [load_whole(bottom_hbm, bottom, 0), load_whole(partner_hbm, partner, 6)]
    top_rows = load_whole(v_hbm.at[:, pl.ds(rows - 8, 8)], v_top, 7)
    first = [
        [load_part(s, t, i, part) for s, t, i in ((land_hbm, land, 1), (diff_hbm, diff, 4), (cot_hbm, cot, 5))]
        for part in range(CHUNKS)
    ]
    second = [
        [load_part(s, t, i, part) for s, t, i in ((u_hbm, u, 2), (v_hbm, v, 3))]
        for part in range(CHUNKS)
    ]
    for copies in [whole] + first + [[top_rows]] + second:
        for copy in copies:
            copy.start()

    lane = lax.broadcasted_iota(jnp.int32, (rows, cols), 1)
    row = lax.broadcasted_iota(jnp.int32, (rows, cols), 0)
    row_last = row == rows - 1
    lane_first, lane_last = lane == 0, lane == cols - 1
    lane_even = lax.rem(lane, 2) == 0
    lane_slot = lax.rem(lane + 1, cols) // 2
    zero = jnp.minimum(lat, 0)
    here = pl.ds(PAD, rows)
    one_north = pl.ds(PAD + 1 + zero, rows)
    one_south = pl.ds(PAD - 1 + zero, rows)
    row_low = lax.broadcasted_iota(jnp.int32, (8, cols), 0)
    low_first, low_last = row_low == 0, row_low == 7

    parts = row_send_sem.shape[2]
    part_rows = 2 * levels // parts

    def row_piece(turn, part):
        return pl.ds(0, levels) if turn == 0 else pl.ds(part * part_rows, part_rows)

    def row_parts(turn):
        return range(1 if turn == 0 else parts)

    def row_copy(turn, part, source_slot, target_slot, device):
        piece = row_piece(turn, part)
        return pltpu.make_async_remote_copy(
            src_ref=row_send.at[turn, source_slot, piece],
            dst_ref=row_recv.at[turn, target_slot, piece],
            send_sem=row_send_sem.at[turn, source_slot, part],
            recv_sem=row_recv_sem.at[turn, target_slot, part],
            device_id=device,
            device_id_type=pl.DeviceIdType.MESH,
        )

    def north_copy(turn, part):
        return row_copy(turn, part, NORTH, north_slot, north)

    def south_copy(turn, part):
        return row_copy(turn, part, SOUTH, NORTH, south)

    def col_copy(turn, source_slot, target_slot, device):
        return pltpu.make_async_remote_copy(
            src_ref=col_send.at[turn, source_slot],
            dst_ref=col_recv.at[turn, target_slot],
            send_sem=col_send_sem.at[turn, source_slot],
            recv_sem=col_recv_sem.at[turn, target_slot],
            device_id=device,
            device_id_type=pl.DeviceIdType.MESH,
        )

    def col_copies(turn):
        return col_copy(turn, EAST, WEST, east), col_copy(turn, WEST, EAST, west)

    def start_rows(turn, part):
        if turn == 0:

            @pl.when(jnp.logical_not(is_top))
            def _():
                north_copy(turn, part).start()

        else:
            north_copy(turn, part).start()

        @pl.when(has_south)
        def _():
            south_copy(turn, part).start()

    def start_cols(turn):
        for copy in col_copies(turn):
            copy.start()

    def wait_recv(turn):
        for slot in (EAST, WEST):
            pltpu.make_async_copy(
                col_recv.at[turn, slot], col_recv.at[turn, slot], col_recv_sem.at[turn, slot]
            ).wait()

        def arrived(slot):
            for part in row_parts(turn):
                piece = row_recv.at[turn, slot, row_piece(turn, part)]
                pltpu.make_async_copy(piece, piece, row_recv_sem.at[turn, slot, part]).wait()

        if turn == 0:

            @pl.when(jnp.logical_not(is_top))
            def _():
                arrived(NORTH)

        else:
            arrived(NORTH)

        @pl.when(has_south)
        def _():
            arrived(SOUTH)

    def wait_sent(turn):
        for copy in col_copies(turn):
            copy.wait_send()

        def left():
            for part in row_parts(turn):
                north_copy(turn, part).wait_send()

        if turn == 0:
            pl.when(jnp.logical_not(is_top))(left)
        else:
            left()

        @pl.when(has_south)
        def _():
            for part in row_parts(turn):
                south_copy(turn, part).wait_send()

    @pl.when(jnp.logical_not(has_south))
    def _():
        for turn in range(3):
            row_recv[turn, SOUTH] = jnp.zeros(row_recv.shape[2:], jnp.float32)

    @pl.when(is_top)
    def _():
        row_recv[0, NORTH] = jnp.zeros(row_recv.shape[2:], jnp.float32)

    no_row = jnp.zeros((1, cols), jnp.float32)

    def looped(start, stop, unroll, body, carry):
        if unroll >= stop - start:
            for level in range(start, stop):
                carry = body(level, carry)
            return carry

        def outer(index, carried):
            for step in range(unroll):
                carried = body(start + index * unroll + step, carried)
            return carried

        return lax.fori_loop(0, (stop - start) // unroll, outer, carry)

    def packed(level, tracer, value, to_west, to_east):
        place = 2 * level + tracer
        turned = pltpu.roll(value, place, 1)
        to_west = jnp.where(lane == place, turned, to_west)
        to_east = jnp.where(lane == (place + cols - 1) % cols, turned, to_east)
        return to_west, to_east

    def gathered(level, value, kept):
        return jnp.where(lane_slot == level, pltpu.roll(value, 2 * level, 1), kept)

    def parted(first_kept, second_kept):
        moved = pltpu.roll(second_kept, 1, 1)
        return jnp.where(lane_even, first_kept, moved), jnp.where(lane_even, moved, first_kept)

    empty = jnp.zeros((rows, cols), jnp.float32)

    load_whole(bottom_hbm, bottom, 0).wait()

    one_row = jnp.ones((1, cols), jnp.float32)

    def flag_of(level):
        flag = jnp.where(level < bottom[...], land[level], 0).astype(jnp.float32)
        wet[level, here] = flag
        return flag

    def factor_level(level, carry):
        above, flag, before = carry
        if level + 1 < levels:
            next_flag = flag_of(level + 1)
            below = diff[level + 1] * (flag * next_flag)
        else:
            next_flag, below = empty, empty
        after = []
        for tracer, ratio in enumerate(RATIOS):
            last_q, last_z = before[tracer]
            up, down = ratio * above, ratio * below
            inverse = 1.0 / (1.0 + up + down - up * last_q)
            q = down * inverse
            z = cot[level, tracer] + last_q * last_z
            big_q[level, tracer] = q
            big_i[level, tracer] = flag * inverse
            z_field[level, tracer] = z
            after.append((q, z))
            x_field[level, tracer, pl.ds(PAD - 1, 1)] = no_row
            x_field[level, tracer, pl.ds(PAD + rows, 1)] = no_row
        wet[level, pl.ds(PAD + rows, 1)] = one_row
        lean_v[level, pl.ds(PAD - 1, 1)] = one_row
        return below, next_flag, tuple(after)

    done = 0
    for part in range(CHUNKS):
        for copy in first[part]:
            copy.wait()
        if part == 0:
            carry = (empty, flag_of(0), ((empty, empty), (empty, empty)))
        stop = levels if part + 1 == CHUNKS else (part + 1) * per_chunk - 1
        carry = looped(done, stop, UNROLL, factor_level, carry)
        done = stop

    def upward(turn):
        def level_up(index, carry):
            level = levels - 1 - index
            after, kept = carry
            fields, edges = [], []
            lean = wet[level, pl.ds(PAD + rows - 8, 8)] * (
                LATERAL_MIX - jnp.minimum(v_top[level], 0.0)
            )
            for tracer in range(2):
                x = (
                    z_field[level, tracer] * big_i[level, tracer]
                    + big_q[level, tracer] * after[tracer]
                )
                x_field[level, tracer, here] = x
                edges.append(gathered(level, x, kept[tracer]))
                weighted = lean * x[rows - 8 :]
                row_send[turn, NORTH, pl.ds(2 * level + tracer, 1), :] = weighted[7:]
                row_send[turn, SOUTH, pl.ds(2 * level + tracer, 1), :] = x[:1]
                fields.append(x)
            return tuple(fields), tuple(edges)

        carry = ((empty, empty), (empty, empty))
        span = levels // parts
        for part in reversed(range(parts)):
            first_index = (parts - 1 - part) * span
            carry = looped(first_index, first_index + span, span // UP_CUT, level_up, carry)
            start_rows(turn, part)
        col_send[turn, WEST], col_send[turn, EAST] = parted(*carry[1])
        start_cols(turn)

    load_whole(partner_hbm, partner, 6).wait()
    picks = jnp.where(
        is_top, partner[...] - mirror * cols, lax.broadcasted_iota(jnp.int32, (1, cols), 1)
    )
    picks = jnp.broadcast_to(picks, (2 * levels, cols))

    def received(turn):
        wait_recv(turn)
        if turn > 0:
            north_rows[turn] = jnp.take_along_axis(
                row_recv[turn, NORTH], picks, axis=1, mode="promise_in_bounds"
            )
        from_east = pltpu.roll(col_recv[turn, EAST], cols - 1, 1)
        from_west = pltpu.roll(col_recv[turn, WEST], 1, 1)
        return (
            jnp.where(lane_even, from_west, from_east),
            jnp.where(lane_even, from_east, from_west),
        )

    def back(level, tracer=0):
        return (cols - (2 * level + tracer)) % cols

    def interior(level, tracer, weights):
        mid, e, w, n, s = weights
        x = x_field[level, tracer, here]
        return (
            mid * x
            + (e * pltpu.roll(x, cols - 1, 1) + w * pltpu.roll(x, 1, 1))
            + (n * x_field[level, tracer, one_north] + s * x_field[level, tracer, one_south])
        )

    top_rows.wait()
    pl.semaphore_wait(barrier, jnp.where(has_south, 4, 3))
    upward(1)

    def static_level(level, carry):
        to_west, to_east = carry
        flag = wet[level, here]
        lean_u = flag * (LATERAL_MIX - jnp.minimum(u[level], 0.0))
        lean = flag * (LATERAL_MIX - jnp.minimum(v[level], 0.0))
        lean_v[level, here] = lean
        row_send[0, NORTH, pl.ds(level, 1), :] = lean[rows - 1 :]
        row_send[0, SOUTH, pl.ds(level, 1), :] = flag[:1]
        edges = jnp.where(lane < cols // 2, flag, lean_u)
        return packed(level, 0, edges, to_west, to_east)

    for copies in second:
        for copy in copies:
            copy.wait()
    col_send[0, WEST], col_send[0, EAST] = looped(0, levels, UNROLL, static_level, (empty, empty))
    start_rows(0, 0)
    start_cols(0)

    first_lane = jnp.where(lane_first, 1.0, 0.0)

    def weights_level(level, carry):
        flag, u_here = wet[level, here], u[level]
        lean_u = flag * (LATERAL_MIX - jnp.minimum(u_here, 0.0))
        drift_u = flag * (jnp.maximum(u_here, 0.0) + LATERAL_MIX)
        e = drift_u * jnp.where(lane_last, 0.0, pltpu.roll(flag, cols - 1, 1))
        w = flag * jnp.where(lane_first, 0.0, pltpu.roll(lean_u, 1, 1))
        n = flag * wet[level, one_north] * (jnp.maximum(v[level], 0.0) + LATERAL_MIX)
        s = flag * lean_v[level, one_south]
        both = n + s
        both = jnp.concatenate(
            [
                jnp.where(low_first, n[:8], both[:8]),
                both[8 : rows - 8],
                jnp.where(low_last, s[rows - 8 :], both[rows - 8 :]),
            ],
            axis=0,
        )
        mid = ((1.0 - e) - w) - both
        c_mid[level] = mid
        c_east[level] = e
        c_west[level] = w
        c_north[level] = n
        c_south[level] = s
        c_edge[level] = jnp.where(lane_last, drift_u, first_lane * flag)
        for tracer in range(2):
            z_field[level, tracer] = interior(level, tracer, (mid, e, w, n, s))
        return carry

    looped(0, levels, W_UNROLL, weights_level, 0)

    first_edges = received(1)
    static_edges, _ = received(0)
    own_west, own_east = col_send[1, WEST], col_send[1, EAST]
    first_edges = (
        static_edges * (first_edges[0] - jnp.where(lane_even, own_west, own_east)),
        pltpu.roll(static_edges, 1, 1)
        * (first_edges[1] - jnp.where(lane_even, own_east, own_west)),
    )

    def row_weights(level):
        north_flag = row_recv[0, NORTH, pl.ds(level, 1), :]
        cut_n, cut_s = c_north[level, rows - 8 :], c_south[level, :8]
        mid_n = jnp.where(low_last, cut_n * jnp.where(is_top, 1.0, north_flag), 0.0)
        mid_s = jnp.where(low_first, cut_s * row_recv[0, SOUTH, pl.ds(level, 1), :], 0.0)
        whole_n = jnp.where(
            is_top, wet[level, pl.ds(PAD + rows - 8, 8)], cut_n * north_flag
        )
        return cut_n, cut_s, mid_n, mid_s, whole_n

    def down_level(level, carry):
        _, cut_s, mid_n, mid_s, whole_n = row_weights(level)
        edge = c_edge[level]
        after = []
        for tracer in range(2):
            last_q, last_z = carry[tracer]
            place = pl.ds(2 * level + tracer, 1)
            turned = pltpu.roll(first_edges[tracer], back(level, tracer), 1)
            total = (z_field[level, tracer] + last_q * last_z) + edge * turned
            x_n = x_field[level, tracer, pl.ds(PAD + rows - 8, 8)]
            x_s = x_field[level, tracer, pl.ds(PAD, 8)]
            at_n = jnp.where(low_last, whole_n * north_rows[1, place, :], 0.0) - mid_n * x_n
            at_s = jnp.where(low_first, cut_s * row_recv[1, SOUTH, place, :], 0.0) - mid_s * x_s
            z = jnp.concatenate(
                [total[:8] + at_s, total[8 : rows - 8], total[rows - 8 :] + at_n], axis=0
            )
            z_field[level, tracer] = z
            after.append((big_q[level, tracer], z))
        return tuple(after)

    looped(0, levels, UNROLL, down_level, ((empty, empty), (empty, empty)))
    upward(2)

    def interior_level(level, carry):
        cut_n, _, mid_n, mid_s, whole_n = row_weights(level)
        edge = c_edge[level] * pltpu.roll(static_edges, back(level), 1)
        c_edge[level] = edge
        mid = c_mid[level] - edge
        mid = jnp.concatenate(
            [mid[:8] - mid_s, mid[8 : rows - 8], mid[rows - 8 :] - mid_n], axis=0
        )
        weights = mid, c_east[level], c_west[level], c_north[level], c_south[level]
        c_north[level, rows - 8 :] = jnp.where(low_last, whole_n, cut_n)
        for tracer in range(2):
            out[level, tracer] = interior(level, tracer, weights)
        return carry

    looped(0, levels, UNROLL, interior_level, 0)
    out_edges[0], out_edges[1] = received(2)
    out_rows[NORTH] = north_rows[2]
    out_rows[SOUTH] = row_recv[2, SOUTH]
    for turn in range(3):
        wait_sent(turn)


def finish_body(part, c_edge, c_north, c_south, edges, rows_in, out_hbm, out, out_sem):
    levels, _, rows, cols = part.shape
    row_low = lax.broadcasted_iota(jnp.int32, (8, cols), 0)
    low_first, low_last = row_low == 0, row_low == 7
    per_chunk = levels // OUT_CHUNKS

    def copy(chunk):
        piece = pl.ds(chunk * per_chunk, per_chunk)
        return pltpu.make_async_copy(out.at[piece], out_hbm.at[piece], out_sem.at[chunk])

    for level in range(levels):
        for tracer in range(2):
            place = 2 * level + tracer
            turned = pltpu.roll(edges[tracer], (cols - place) % cols, 1)
            total = part[level, tracer] + c_edge[level] * turned
            n = c_north[level, rows - 8 :] * rows_in[NORTH, pl.ds(place, 1), :]
            s = c_south[level, :8] * rows_in[SOUTH, pl.ds(place, 1), :]
            out[level, tracer, :8] = total[:8] + jnp.where(low_first, s, 0.0)
            out[level, tracer, 8 : rows - 8] = total[8 : rows - 8]
            out[level, tracer, rows - 8 :] = total[rows - 8 :] + jnp.where(low_last, n, 0.0)
        if (level + 1) % per_chunk == 0:
            copy(level // per_chunk).start()
    for chunk in range(OUT_CHUNKS):
        copy(chunk).wait()


def per_device(cotangent, u_transport, v_transport, diffusivity, land_sea, bottom_level, partner):
    levels, rows, cols = u_transport.shape
    level_field = pltpu.VMEM((levels, rows, cols), jnp.float32)
    pair_field = pltpu.VMEM((levels, 2, rows, cols), jnp.float32)
    anywhere = pl.BlockSpec(memory_space=pl.ANY)
    whole = pl.BlockSpec(memory_space=pltpu.VMEM)
    parts = pl.pallas_call(
        kernel_body,
        out_shape=[
            pair_field,
            level_field,
            level_field,
            level_field,
            pltpu.VMEM((2, rows, cols), jnp.float32),
            pltpu.VMEM((2, 2 * levels, cols), jnp.float32),
        ],
        in_specs=[anywhere] * 7,
        out_specs=[whole] * 6,
        scratch_shapes=[
            pair_field,
            level_field,
            level_field,
            level_field,
            pltpu.VMEM((levels, rows, cols), jnp.int32),
            pltpu.VMEM((rows, cols), jnp.int32),
            pltpu.VMEM((1, cols), jnp.int32),
            pltpu.VMEM((levels, rows + 2 * PAD, cols), jnp.float32),
            pltpu.VMEM((levels, rows + 2 * PAD, cols), jnp.float32),
            pair_field,
            pair_field,
            pltpu.VMEM((levels, 2, rows + 2 * PAD, cols), jnp.float32),
            pair_field,
            level_field,
            level_field,
            level_field,
            pltpu.VMEM((3, 2, 2 * levels, cols), jnp.float32),
            pltpu.VMEM((3, 2, 2 * levels, cols), jnp.float32),
            pltpu.VMEM((3, 2, rows, cols), jnp.float32),
            pltpu.VMEM((3, 2, rows, cols), jnp.float32),
            pltpu.VMEM((3, 2 * levels, cols), jnp.float32),
            pltpu.VMEM((levels, 8, cols), jnp.float32),
            pltpu.SemaphoreType.DMA((8, CHUNKS)),
            pltpu.SemaphoreType.DMA((3, 2, ROW_PARTS)),
            pltpu.SemaphoreType.DMA((3, 2, ROW_PARTS)),
            pltpu.SemaphoreType.DMA((3, 2)),
            pltpu.SemaphoreType.DMA((3, 2)),
        ],
        compiler_params=pltpu.CompilerParams(
            collective_id=0, has_side_effects=True, vmem_limit_bytes=30 << 20
        ),
    )(
        *(
            pltpu.with_memory_space_constraint(array, pltpu.HBM)
            for array in (
                cotangent,
                u_transport,
                v_transport,
                diffusivity,
                land_sea,
                bottom_level,
                partner[None, :],
            )
        )
    )
    return pl.pallas_call(
        finish_body,
        out_shape=jax.ShapeDtypeStruct(cotangent.shape, jnp.float32),
        in_specs=[whole] * 6,
        out_specs=anywhere,
        scratch_shapes=[pair_field, pltpu.SemaphoreType.DMA((OUT_CHUNKS,))],
        compiler_params=pltpu.CompilerParams(vmem_limit_bytes=30 << 20),
    )(*parts)


def solution(mesh):
    placed = (
        P(None, None, "lat", "lon"),
        P(None, "lat", "lon"),
        P(None, "lat", "lon"),
        P(None, "lat", "lon"),
        P(None, "lat", "lon"),
        P("lat", "lon"),
        P("lon"),
    )
    return jax.shard_map(
        per_device,
        mesh=mesh,
        in_specs=placed,
        out_specs=P(None, None, "lat", "lon"),
        check_vma=False,
    )
```

```python
import functools

import jax
import jax.numpy as jnp
from jax import lax
from jax.experimental import pallas as pl
from jax.experimental.pallas import tpu as pltpu
from jax.sharding import PartitionSpec as P

LATERAL_MIX = 0.15
SALT_RATIO = 0.5
UNROLL = 40
W_UNROLL = 20
UP_CUT = 1
ROW_PARTS = 2
FIRST_ROWS = 20
RATIOS = (1.0, SALT_RATIO)
NORTH, SOUTH = range(2)
EAST, WEST = range(2)
CHUNKS = 5
OUT_CHUNKS = 5
PAD = 8


def kernel_body(
    cot_hbm, u_hbm, v_hbm, diff_hbm, land_hbm, bottom_hbm, partner_hbm,
    out, c_edge, c_north, c_south, out_edges, out_rows,
    cot, u, v, diff, land, bottom, partner, wet, lean_v, big_q, big_i, x_field, z_field,
    c_mid, c_east, c_west,
    row_send, row_recv, col_send, col_recv, north_rows, v_top,
    in_sem, row_send_sem, row_recv_sem, col_send_sem, col_recv_sem,
):
    levels, rows, cols = u.shape
    per_chunk = levels // CHUNKS
    lat, lon = lax.axis_index("lat"), lax.axis_index("lon")
    lats, lons = lax.axis_size("lat"), lax.axis_size("lon")
    is_top = lat == lats - 1
    has_south = lat > 0
    mirror = lons - 1 - lon
    east = (lat, lax.rem(lon + 1, lons))
    west = (lat, lax.rem(lon + lons - 1, lons))
    north = (jnp.where(is_top, lat, lat + 1), jnp.where(is_top, mirror, lon))
    south = (jnp.maximum(lat - 1, 0), lon)
    north_slot = jnp.where(is_top, NORTH, SOUTH)

    def signal(device):
        pl.semaphore_signal(
            barrier, inc=1, device_id=device, device_id_type=pl.DeviceIdType.MESH
        )

    barrier = pltpu.get_barrier_semaphore()
    signal(east)
    signal(west)
    signal(north)

    @pl.when(has_south)
    def _():
        signal(south)

    def load_whole(source, target, index):
        return pltpu.make_async_copy(source, target, in_sem.at[index, 0])

    def load_part(source, target, index, part):
        piece = pl.ds(part * per_chunk, per_chunk)
        return pltpu.make_async_copy(source.at[piece], target.at[piece], in_sem.at[index, part])

    whole = [load_whole(bottom_hbm, bottom, 0), load_whole(partner_hbm, partner, 6)]
    top_rows = load_whole(v_hbm.at[:, pl.ds(rows - 8, 8)], v_top, 7)
    first = [
        [load_part(s, t, i, part) for s, t, i in ((land_hbm, land, 1), (diff_hbm, diff, 4), (cot_hbm, cot, 5))]
        for part in range(CHUNKS)
    ]
    second = [
        [load_part(s, t, i, part) for s, t, i in ((u_hbm, u, 2), (v_hbm, v, 3))]
        for part in range(CHUNKS)
    ]
    for copies in [whole, first[0], [top_rows]] + first[1:] + second:
        for copy in copies:
            copy.start()

    lane = lax.broadcasted_iota(jnp.int32, (rows, cols), 1)
    row = lax.broadcasted_iota(jnp.int32, (rows, cols), 0)
    row_last = row == rows - 1
    lane_first, lane_last = lane == 0, lane == cols - 1
    lane_even = lax.rem(lane, 2) == 0
    lane_slot = lax.rem(lane + 1, cols) // 2
    zero = jnp.minimum(lat, 0)
    here = pl.ds(PAD, rows)
    one_north = pl.ds(PAD + 1 + zero, rows)
    one_south = pl.ds(PAD - 1 + zero, rows)
    row_low = lax.broadcasted_iota(jnp.int32, (8, cols), 0)
    low_first, low_last = row_low == 0, row_low == 7

    parts = row_send_sem.shape[2]
    bounds = (0, FIRST_ROWS, levels)

    def row_piece(turn, part):
        return (
            pl.ds(0, levels)
            if turn == 0
            else pl.ds(2 * bounds[part], 2 * (bounds[part + 1] - bounds[part]))
        )

    def row_parts(turn):
        return range(1 if turn == 0 else parts)

    def row_copy(turn, part, source_slot, target_slot, device):
        piece = row_piece(turn, part)
        return pltpu.make_async_remote_copy(
            src_ref=row_send.at[turn, source_slot, piece],
            dst_ref=row_recv.at[turn, target_slot, piece],
            send_sem=row_send_sem.at[turn, source_slot, part],
            recv_sem=row_recv_sem.at[turn, target_slot, part],
            device_id=device,
            device_id_type=pl.DeviceIdType.MESH,
        )

    def north_copy(turn, part):
        return row_copy(turn, part, NORTH, north_slot, north)

    def south_copy(turn, part):
        return row_copy(turn, part, SOUTH, NORTH, south)

    def col_copy(turn, source_slot, target_slot, device):
        return pltpu.make_async_remote_copy(
            src_ref=col_send.at[turn, source_slot],
            dst_ref=col_recv.at[turn, target_slot],
            send_sem=col_send_sem.at[turn, source_slot],
            recv_sem=col_recv_sem.at[turn, target_slot],
            device_id=device,
            device_id_type=pl.DeviceIdType.MESH,
        )

    def col_copies(turn):
        return col_copy(turn, EAST, WEST, east), col_copy(turn, WEST, EAST, west)

    def start_rows(turn, part):
        if turn == 0:

            @pl.when(jnp.logical_not(is_top))
            def _():
                north_copy(turn, part).start()

        else:
            north_copy(turn, part).start()

        @pl.when(has_south)
        def _():
            south_copy(turn, part).start()

    def start_cols(turn):
        for copy in col_copies(turn):
            copy.start()

    def wait_recv(turn):
        for slot in (EAST, WEST):
            pltpu.make_async_copy(
                col_recv.at[turn, slot], col_recv.at[turn, slot], col_recv_sem.at[turn, slot]
            ).wait()

        def arrived(slot):
            for part in row_parts(turn):
                piece = row_recv.at[turn, slot, row_piece(turn, part)]
                pltpu.make_async_copy(piece, piece, row_recv_sem.at[turn, slot, part]).wait()

        if turn == 0:

            @pl.when(jnp.logical_not(is_top))
            def _():
                arrived(NORTH)

        else:
            arrived(NORTH)

        @pl.when(has_south)
        def _():
            arrived(SOUTH)

    def wait_sent(turn):
        for copy in col_copies(turn):
            copy.wait_send()

        def left():
            for part in row_parts(turn):
                north_copy(turn, part).wait_send()

        if turn == 0:
            pl.when(jnp.logical_not(is_top))(left)
        else:
            left()

        @pl.when(has_south)
        def _():
            for part in row_parts(turn):
                south_copy(turn, part).wait_send()

    @pl.when(jnp.logical_not(has_south))
    def _():
        for turn in range(3):
            row_recv[turn, SOUTH] = jnp.zeros(row_recv.shape[2:], jnp.float32)

    @pl.when(is_top)
    def _():
        row_recv[0, NORTH] = jnp.zeros(row_recv.shape[2:], jnp.float32)

    no_row = jnp.zeros((1, cols), jnp.float32)

    def looped(start, stop, unroll, body, carry):
        if unroll >= stop - start:
            for level in range(start, stop):
                carry = body(level, carry)
            return carry

        def outer(index, carried):
            for step in range(unroll):
                carried = body(start + index * unroll + step, carried)
            return carried

        return lax.fori_loop(0, (stop - start) // unroll, outer, carry)

    def packed(level, tracer, value, to_west, to_east):
        place = 2 * level + tracer
        turned = pltpu.roll(value, place, 1)
        to_west = jnp.where(lane == place, turned, to_west)
        to_east = jnp.where(lane == (place + cols - 1) % cols, turned, to_east)
        return to_west, to_east

    def gathered(level, value, kept):
        return jnp.where(lane_slot == level, pltpu.roll(value, 2 * level, 1), kept)

    def parted(first_kept, second_kept):
        moved = pltpu.roll(second_kept, 1, 1)
        return jnp.where(lane_even, first_kept, moved), jnp.where(lane_even, moved, first_kept)

    empty = jnp.zeros((rows, cols), jnp.float32)

    load_whole(bottom_hbm, bottom, 0).wait()

    one_row = jnp.ones((1, cols), jnp.float32)

    def flag_of(level):
        flag = jnp.where(level < bottom[...], land[level], 0).astype(jnp.float32)
        wet[level, here] = flag
        return flag

    def factor_level(level, carry):
        flag, before = carry
        if level + 1 < levels:
            next_flag = flag_of(level + 1)
            below = diff[level + 1] * (flag * next_flag)
        else:
            next_flag, below = empty, empty
        after = []
        for tracer, ratio in enumerate(RATIOS):
            pivot, passed = before[tracer]
            down = ratio * below
            inverse = 1.0 / (pivot + down)
            q = down * inverse
            z = cot[level, tracer] + passed
            big_q[level, tracer] = q
            big_i[level, tracer] = flag * inverse
            z_field[level, tracer] = z
            after.append((1.0 + pivot * q, q * z))
            x_field[level, tracer, pl.ds(PAD - 1, 1)] = no_row
            x_field[level, tracer, pl.ds(PAD + rows, 1)] = no_row
        wet[level, pl.ds(PAD + rows, 1)] = one_row
        lean = flag[rows - 8 :] * (LATERAL_MIX - jnp.minimum(v_top[level], 0.0))
        row_send[0, NORTH, pl.ds(level, 1), :] = lean[7:]
        row_send[0, SOUTH, pl.ds(level, 1), :] = flag[:1]
        lean_v[level, pl.ds(PAD - 1, 1)] = one_row
        return next_flag, tuple(after)

    ones = jnp.ones((rows, cols), jnp.float32)
    done = 0
    for part in range(CHUNKS):
        for copy in first[part]:
            copy.wait()
        if part == 0:
            top_rows.wait()
            carry = (flag_of(0), ((ones, empty), (ones, empty)))
        stop = levels if part + 1 == CHUNKS else (part + 1) * per_chunk - 1
        carry = looped(done, stop, UNROLL, factor_level, carry)
        done = stop

    def upward(turn):
        def level_up(index, carry):
            level = levels - 1 - index
            after, kept = carry
            fields, edges = [], []
            lean = wet[level, pl.ds(PAD + rows - 8, 8)] * (
                LATERAL_MIX - jnp.minimum(v_top[level], 0.0)
            )
            for tracer in range(2):
                x = (
                    z_field[level, tracer] * big_i[level, tracer]
                    + big_q[level, tracer] * after[tracer]
                )
                x_field[level, tracer, here] = x
                edges.append(gathered(level, x, kept[tracer]))
                weighted = lean * x[rows - 8 :]
                row_send[turn, NORTH, pl.ds(2 * level + tracer, 1), :] = weighted[7:]
                row_send[turn, SOUTH, pl.ds(2 * level + tracer, 1), :] = x[:1]
                fields.append(x)
            return tuple(fields), tuple(edges)

        carry = ((empty, empty), (empty, empty))
        for part in reversed(range(parts)):
            for index in range(levels - bounds[part + 1], levels - bounds[part]):
                carry = level_up(index, carry)
            start_rows(turn, part)
        col_send[turn, WEST], col_send[turn, EAST] = parted(*carry[1])
        start_cols(turn)

    load_whole(partner_hbm, partner, 6).wait()
    picks = jnp.where(
        is_top, partner[...] - mirror * cols, lax.broadcasted_iota(jnp.int32, (1, cols), 1)
    )
    picks = jnp.broadcast_to(picks, (2 * levels, cols))

    def received(turn):
        wait_recv(turn)
        if turn > 0:
            north_rows[turn] = jnp.take_along_axis(
                row_recv[turn, NORTH], picks, axis=1, mode="promise_in_bounds"
            )
        from_east = pltpu.roll(col_recv[turn, EAST], cols - 1, 1)
        from_west = pltpu.roll(col_recv[turn, WEST], 1, 1)
        return (
            jnp.where(lane_even, from_west, from_east),
            jnp.where(lane_even, from_east, from_west),
        )

    def back(level, tracer=0):
        return (cols - (2 * level + tracer)) % cols

    def interior(level, tracer, weights):
        mid, e, w, n, s = weights
        x = x_field[level, tracer, here]
        return (
            mid * x
            + (e * pltpu.roll(x, cols - 1, 1) + w * pltpu.roll(x, 1, 1))
            + (n * x_field[level, tracer, one_north] + s * x_field[level, tracer, one_south])
        )

    pl.semaphore_wait(barrier, jnp.where(has_south, 4, 3))
    start_rows(0, 0)
    upward(1)

    def static_level(level, kept):
        flag = wet[level, here]
        lean_u = flag * (LATERAL_MIX - jnp.minimum(u[level], 0.0))
        lean = flag * (LATERAL_MIX - jnp.minimum(v[level], 0.0))
        lean_v[level, here] = lean
        edges = jnp.where(lane < cols // 2, flag, lean_u)
        return gathered(level, edges, kept)

    for copies in second:
        for copy in copies:
            copy.wait()
    kept = looped(0, levels, UNROLL, static_level, empty)
    col_send[0, WEST] = kept
    col_send[0, EAST] = kept
    start_cols(0)

    first_lane = jnp.where(lane_first, 1.0, 0.0)

    def weights_level(level, carry):
        flag, u_here = wet[level, here], u[level]
        lean_u = flag * (LATERAL_MIX - jnp.minimum(u_here, 0.0))
        drift_u = flag * (jnp.maximum(u_here, 0.0) + LATERAL_MIX)
        e = drift_u * jnp.where(lane_last, 0.0, pltpu.roll(flag, cols - 1, 1))
        w = flag * jnp.where(lane_first, 0.0, pltpu.roll(lean_u, 1, 1))
        n = flag * wet[level, one_north] * (jnp.maximum(v[level], 0.0) + LATERAL_MIX)
        s = flag * lean_v[level, one_south]
        both = n + s
        both = jnp.concatenate(
            [
                jnp.where(low_first, n[:8], both[:8]),
                both[8 : rows - 8],
                jnp.where(low_last, s[rows - 8 :], both[rows - 8 :]),
            ],
            axis=0,
        )
        mid = ((1.0 - e) - w) - both
        c_mid[level] = mid
        c_east[level] = e
        c_west[level] = w
        c_north[level] = n
        c_south[level] = s
        c_edge[level] = jnp.where(lane_last, drift_u, first_lane * flag)
        for tracer in range(2):
            z_field[level, tracer] = interior(level, tracer, (mid, e, w, n, s))
        return carry

    looped(0, levels, W_UNROLL, weights_level, 0)

    first_edges = received(1)
    static_edges, _ = received(0)
    own_west, own_east = col_send[1, WEST], col_send[1, EAST]
    first_edges = (
        static_edges * (first_edges[0] - jnp.where(lane_even, own_west, own_east)),
        pltpu.roll(static_edges, 1, 1)
        * (first_edges[1] - jnp.where(lane_even, own_east, own_west)),
    )

    def row_weights(level):
        north_flag = row_recv[0, NORTH, pl.ds(level, 1), :]
        cut_n, cut_s = c_north[level, rows - 8 :], c_south[level, :8]
        mid_n = jnp.where(low_last, cut_n * jnp.where(is_top, 1.0, north_flag), 0.0)
        mid_s = jnp.where(low_first, cut_s * row_recv[0, SOUTH, pl.ds(level, 1), :], 0.0)
        whole_n = jnp.where(
            is_top, wet[level, pl.ds(PAD + rows - 8, 8)], cut_n * north_flag
        )
        return cut_n, cut_s, mid_n, mid_s, whole_n

    def down_level(level, carry):
        _, cut_s, mid_n, mid_s, whole_n = row_weights(level)
        edge = c_edge[level]
        after = []
        for tracer in range(2):
            last_q, last_z = carry[tracer]
            place = pl.ds(2 * level + tracer, 1)
            turned = pltpu.roll(first_edges[tracer], back(level, tracer), 1)
            total = (z_field[level, tracer] + last_q * last_z) + edge * turned
            x_n = x_field[level, tracer, pl.ds(PAD + rows - 8, 8)]
            x_s = x_field[level, tracer, pl.ds(PAD, 8)]
            at_n = jnp.where(low_last, whole_n * north_rows[1, place, :], 0.0) - mid_n * x_n
            at_s = jnp.where(low_first, cut_s * row_recv[1, SOUTH, place, :], 0.0) - mid_s * x_s
            z = jnp.concatenate(
                [total[:8] + at_s, total[8 : rows - 8], total[rows - 8 :] + at_n], axis=0
            )
            z_field[level, tracer] = z
            after.append((big_q[level, tracer], z))
        return tuple(after)

    looped(0, levels, UNROLL, down_level, ((empty, empty), (empty, empty)))
    upward(2)

    def interior_level(level, carry):
        cut_n, _, mid_n, mid_s, whole_n = row_weights(level)
        edge = c_edge[level] * pltpu.roll(static_edges, back(level), 1)
        c_edge[level] = edge
        mid = c_mid[level] - edge
        mid = jnp.concatenate(
            [mid[:8] - mid_s, mid[8 : rows - 8], mid[rows - 8 :] - mid_n], axis=0
        )
        weights = mid, c_east[level], c_west[level], c_north[level], c_south[level]
        c_north[level, rows - 8 :] = jnp.where(low_last, whole_n, cut_n)
        for tracer in range(2):
            out[level, tracer] = interior(level, tracer, weights)
        return carry

    looped(0, levels, UNROLL, interior_level, 0)
    out_edges[0], out_edges[1] = received(2)
    out_rows[NORTH] = north_rows[2]
    out_rows[SOUTH] = row_recv[2, SOUTH]
    for turn in range(3):
        wait_sent(turn)


def finish_body(part, c_edge, c_north, c_south, edges, rows_in, out_hbm, out, out_sem):
    levels, _, rows, cols = part.shape
    row_low = lax.broadcasted_iota(jnp.int32, (8, cols), 0)
    low_first, low_last = row_low == 0, row_low == 7
    per_chunk = levels // OUT_CHUNKS

    def copy(chunk):
        piece = pl.ds(chunk * per_chunk, per_chunk)
        return pltpu.make_async_copy(out.at[piece], out_hbm.at[piece], out_sem.at[chunk])

    for level in range(levels):
        for tracer in range(2):
            place = 2 * level + tracer
            turned = pltpu.roll(edges[tracer], (cols - place) % cols, 1)
            total = part[level, tracer] + c_edge[level] * turned
            n = c_north[level, rows - 8 :] * rows_in[NORTH, pl.ds(place, 1), :]
            s = c_south[level, :8] * rows_in[SOUTH, pl.ds(place, 1), :]
            out[level, tracer, :8] = total[:8] + jnp.where(low_first, s, 0.0)
            out[level, tracer, 8 : rows - 8] = total[8 : rows - 8]
            out[level, tracer, rows - 8 :] = total[rows - 8 :] + jnp.where(low_last, n, 0.0)
        if (level + 1) % per_chunk == 0:
            copy(level // per_chunk).start()
    for chunk in range(OUT_CHUNKS):
        copy(chunk).wait()


def per_device(cotangent, u_transport, v_transport, diffusivity, land_sea, bottom_level, partner):
    levels, rows, cols = u_transport.shape
    level_field = pltpu.VMEM((levels, rows, cols), jnp.float32)
    pair_field = pltpu.VMEM((levels, 2, rows, cols), jnp.float32)
    anywhere = pl.BlockSpec(memory_space=pl.ANY)
    whole = pl.BlockSpec(memory_space=pltpu.VMEM)
    parts = pl.pallas_call(
        kernel_body,
        out_shape=[
            pair_field,
            level_field,
            level_field,
            level_field,
            pltpu.VMEM((2, rows, cols), jnp.float32),
            pltpu.VMEM((2, 2 * levels, cols), jnp.float32),
        ],
        in_specs=[anywhere] * 7,
        out_specs=[whole] * 6,
        scratch_shapes=[
            pair_field,
            level_field,
            level_field,
            level_field,
            pltpu.VMEM((levels, rows, cols), jnp.int32),
            pltpu.VMEM((rows, cols), jnp.int32),
            pltpu.VMEM((1, cols), jnp.int32),
            pltpu.VMEM((levels, rows + 2 * PAD, cols), jnp.float32),
            pltpu.VMEM((levels, rows + 2 * PAD, cols), jnp.float32),
            pair_field,
            pair_field,
            pltpu.VMEM((levels, 2, rows + 2 * PAD, cols), jnp.float32),
            pair_field,
            level_field,
            level_field,
            level_field,
            pltpu.VMEM((3, 2, 2 * levels, cols), jnp.float32),
            pltpu.VMEM((3, 2, 2 * levels, cols), jnp.float32),
            pltpu.VMEM((3, 2, rows, cols), jnp.float32),
            pltpu.VMEM((3, 2, rows, cols), jnp.float32),
            pltpu.VMEM((3, 2 * levels, cols), jnp.float32),
            pltpu.VMEM((levels, 8, cols), jnp.float32),
            pltpu.SemaphoreType.DMA((8, CHUNKS)),
            pltpu.SemaphoreType.DMA((3, 2, ROW_PARTS)),
            pltpu.SemaphoreType.DMA((3, 2, ROW_PARTS)),
            pltpu.SemaphoreType.DMA((3, 2)),
            pltpu.SemaphoreType.DMA((3, 2)),
        ],
        compiler_params=pltpu.CompilerParams(
            collective_id=0, has_side_effects=True, vmem_limit_bytes=30 << 20
        ),
    )(
        *(
            pltpu.with_memory_space_constraint(array, pltpu.HBM)
            for array in (
                cotangent,
                u_transport,
                v_transport,
                diffusivity,
                land_sea,
                bottom_level,
                partner[None, :],
            )
        )
    )
    return pl.pallas_call(
        finish_body,
        out_shape=jax.ShapeDtypeStruct(cotangent.shape, jnp.float32),
        in_specs=[whole] * 6,
        out_specs=anywhere,
        scratch_shapes=[pair_field, pltpu.SemaphoreType.DMA((OUT_CHUNKS,))],
        compiler_params=pltpu.CompilerParams(vmem_limit_bytes=30 << 20),
    )(*parts)


def solution(mesh):
    placed = (
        P(None, None, "lat", "lon"),
        P(None, "lat", "lon"),
        P(None, "lat", "lon"),
        P(None, "lat", "lon"),
        P(None, "lat", "lon"),
        P("lat", "lon"),
        P("lon"),
    )
    return jax.shard_map(
        per_device,
        mesh=mesh,
        in_specs=placed,
        out_specs=P(None, None, "lat", "lon"),
        check_vma=False,
    )
```
